32 devices in a mesh: parts: 2 (over y), patch: 4 (over z), sub: 2 (over x), lvl: 2 (over core).
Axes of the slice: x: 2, y: 2, z: 4, core: 2. Of those that a mesh axis runs over, the one named last changes fastest.
Arguments:
- node_states: float32 [8192, 512], P(('parts', 'patch', 'lvl')), parts along dimension 0, may hold values from -6 to 6
- coarse_states: float32 [1024, 512], P(('parts', 'patch', 'lvl')), parts along dimension 0, may hold values from -6 to 6
- children: int32 [512, 7], P(('patch', 'lvl')), may hold values from 0 to 511
- down_sources: int32 [4096, 3], P(('patch', 'lvl')), may hold values from 0 to 63
- bottom_links: int32 [4096, 6], P(('patch', 'lvl')), may hold values from 0 to 767, as said below
- coarse_links: int32 [512, 6], P(('patch', 'lvl')), may hold values from 0 to 511
- upward_sender: float32 [512, 512], P(None, 'sub'), may hold values from -0.25 to 0.25
- upward_receiver: float32 [512, 512], P(None, 'sub'), may hold values from -0.25 to 0.25
- upward_bias: float32 [512], P('sub'), may hold values from -4 to 4
- upward_output: float32 [512, 512], P('sub'), may hold values from -0.25 to 0.25
- upward_gain: float32 [512], replicated, may hold values from 0.1 to 1.9
- coarse_sender: float32 [512, 512], P(None, 'sub'), may hold values from -0.25 to 0.25
- coarse_receiver: float32 [512, 512], P(None, 'sub'), may hold values from -0.25 to 0.25
- coarse_bias: float32 [512], P('sub'), may hold values from -4 to 4
- coarse_output: float32 [512, 512], P('sub'), may hold values from -0.25 to 0.25
- coarse_gain: float32 [512], replicated, may hold values from 0.1 to 1.9
- downward_sender: float32 [512, 512], P(None, 'sub'), may hold values from -0.25 to 0.25
- downward_receiver: float32 [512, 512], P(None, 'sub'), may hold values from -0.25 to 0.25
- downward_bias: float32 [512], P('sub'), may hold values from -4 to 4
- downward_output: float32 [512, 512], P('sub'), may hold values from -0.25 to 0.25
- downward_gain: float32 [512], replicated, may hold values from 0.1 to 1.9
- bottom_sender: float32 [512, 512], P(None, 'sub'), may hold values from -0.25 to 0.25
- bottom_receiver: float32 [512, 512], P(None, 'sub'), may hold values from -0.25 to 0.25
- bottom_bias: float32 [512], P('sub'), may hold values from -4 to 4
- bottom_output: float32 [512, 512], P('sub'), may hold values from -0.25 to 0.25
- bottom_gain: float32 [512], replicated, may hold values from 0.1 to 1.9
Outputs:
- new_nodes: float32 [8192, 512], P(('parts', 'patch', 'lvl')), parts along dimension 0
- new_coarse: float32 [1024, 512], P(('parts', 'patch', 'lvl')), parts along dimension 0
The draws below stay inside these ranges and needn't reach their ends.
There are 2 independent parts, one for each index of `parts`. The reference program is written for one: setup_inputs(seed, part) draws one part's arguments, and reference() takes and returns one part's arrays. A program takes and returns all parts, laid end to end along the dimension named above; an argument that names none is the same for every part. Nothing has to cross between parts.
Inputs may be any that keep to these rules, and one draw needn't show every extreme that they name: bottom_links[n, k] - 128 differs from n's row within its block by at most 128.
All inputs are finite; a program needn't handle non-finite values.
Results may differ from the reference program's by a relative error of at most 0.00011.
Values sent between devices are 32-bit elements; how exact they have to be, the bound alone decides.
A program may use at most 64 MiB of HBM per device.

```python
import jax
import jax.numpy as jnp
from jax import lax

LAT = 512
HID = 512
ROWS_DEV = 512
DEG = 6
CDEG = 6
UP = 7
DOWN = 3
HALO = 128
CDEV = 64
NB = 4096
NC = 512


def draw_children(key, part):
    factor = ROWS_DEV // CDEV
    position = jnp.arange(NC, dtype=jnp.int32) % CDEV
    offsets = jax.random.randint(key, (NC, UP), -4, 12, dtype=jnp.int32)
    result = jnp.clip(factor * position[:, None] + offsets, 0, ROWS_DEV - 1)
    result = result.at[0, 0].set(0).at[NC - 1, 0].set(ROWS_DEV - 1)
    return result.astype(jnp.int32)


def draw_down_sources(key, part):
    factor = ROWS_DEV // CDEV
    position = jnp.arange(NB, dtype=jnp.int32) % ROWS_DEV
    offsets = jax.random.randint(key, (NB, DOWN), -1, 2, dtype=jnp.int32)
    result = jnp.clip((position // factor)[:, None] + offsets, 0, CDEV - 1)
    result = result.at[0, 0].set(0).at[NB - 1, 0].set(CDEV - 1)
    return result.astype(jnp.int32)


def draw_bottom_links(key, part):
    position = jnp.arange(NB, dtype=jnp.int32) % ROWS_DEV
    offsets = jax.random.randint(key, (NB, DEG), -HALO, HALO + 1, dtype=jnp.int32)
    offsets = jnp.where(offsets == 0, 1, offsets)
    result = HALO + position[:, None] + offsets
    result = result.at[0, 0].set(0).at[NB - 1, 0].set(ROWS_DEV + 2 * HALO - 1)
    return result.astype(jnp.int32)


def draw_coarse_links(key, part):
    blocks = NC // CDEV
    first_key, second_key = jax.random.split(key)
    within = jax.random.randint(first_key, (NC, CDEG), 0, CDEV, dtype=jnp.int32)
    anywhere = jax.random.randint(second_key, (NC, CDEG), 0, blocks, dtype=jnp.int32)
    owning = (jnp.arange(NC, dtype=jnp.int32) // CDEV)[:, None]
    column = jnp.arange(CDEG, dtype=jnp.int32)[None, :]
    shifted = jnp.where(column == 0, owning, jnp.where(column == 1, owning + 1, jnp.where(column == 2, owning - 1 + blocks, owning + blocks // 2)))
    target = jnp.where(column < 4, shifted % blocks, anywhere)
    result = target * CDEV + within
    result = result.at[0, 0].set(0).at[NC - 1, 0].set(NC - 1)
    return result.astype(jnp.int32)


def block_levels(stream_key, extent, cuts, least, largest):
    loudness, own = 1.0, jax.random.fold_in(stream_key, 6)
    for dim, parts in cuts:
        heights = jnp.exp(jax.random.uniform(jax.random.fold_in(own, dim), (parts,), jnp.float32, least / len(cuts), largest / len(cuts)))
        loudness = loudness * jnp.repeat(heights, extent[dim] // parts).reshape([-1 if axis == dim else 1 for axis in range(len(extent))])
    return loudness


def normal_values(stream_key, extent, deviation, limit, shards=(), kind=jnp.bfloat16):
    factor_of = block_levels(stream_key, extent, shards, -0.22, 0.18) if shards else 1.0
    entries = jax.random.normal(stream_key, extent, jnp.float32) * deviation * factor_of
    return jnp.minimum(jnp.maximum(entries, -limit), limit).astype(kind)


def setup_inputs(seed: int = 0, part: int = 0) -> dict:
    streams_of = jax.random.split(jax.random.key(seed), 27)
    own_keys = jax.random.split(jax.random.fold_in(streams_of[26], part), 27)
    return {
        "node_states": normal_values(own_keys[0], (NB, LAT), 1.0, 6.0, ((0, 8),), jnp.float32),
        "coarse_states": normal_values(own_keys[1], (NC, LAT), 1.0, 6.0, ((0, 8),), jnp.float32),
        "children": draw_children(jax.random.fold_in(streams_of[26], 71), part),
        "down_sources": draw_down_sources(jax.random.fold_in(streams_of[26], 71), part),
        "bottom_links": draw_bottom_links(jax.random.fold_in(streams_of[26], 71), part),
        "coarse_links": draw_coarse_links(jax.random.fold_in(streams_of[26], 71), part),
        "upward_sender": normal_values(streams_of[6], (LAT, HID), LAT ** -0.5, 0.25, ((1, 2),), jnp.float32),
        "upward_receiver": normal_values(streams_of[7], (LAT, HID), LAT ** -0.5, 0.25, ((1, 2),), jnp.float32),
        "upward_bias": normal_values(streams_of[8], (HID,), 1.0, 4.0, ((0, 2),), jnp.float32),
        "upward_output": normal_values(streams_of[9], (HID, LAT), HID ** -0.5, 0.25, ((0, 2),), jnp.float32),
        "upward_gain": jnp.clip(1.0 + 0.18 * jax.random.normal(streams_of[10], (LAT,), jnp.float32), 0.1, 1.9),
        "coarse_sender": normal_values(streams_of[11], (LAT, HID), LAT ** -0.5, 0.25, ((1, 2),), jnp.float32),
        "coarse_receiver": normal_values(streams_of[12], (LAT, HID), LAT ** -0.5, 0.25, ((1, 2),), jnp.float32),
        "coarse_bias": normal_values(streams_of[13], (HID,), 1.0, 4.0, ((0, 2),), jnp.float32),
        "coarse_output": normal_values(streams_of[14], (HID, LAT), HID ** -0.5, 0.25, ((0, 2),), jnp.float32),
        "coarse_gain": jnp.clip(1.0 + 0.18 * jax.random.normal(streams_of[15], (LAT,), jnp.float32), 0.1, 1.9),
        "downward_sender": normal_values(streams_of[16], (LAT, HID), LAT ** -0.5, 0.25, ((1, 2),), jnp.float32),
        "downward_receiver": normal_values(streams_of[17], (LAT, HID), LAT ** -0.5, 0.25, ((1, 2),), jnp.float32),
        "downward_bias": normal_values(streams_of[18], (HID,), 1.0, 4.0, ((0, 2),), jnp.float32),
        "downward_output": normal_values(streams_of[19], (HID, LAT), HID ** -0.5, 0.25, ((0, 2),), jnp.float32),
        "downward_gain": jnp.clip(1.0 + 0.18 * jax.random.normal(streams_of[20], (LAT,), jnp.float32), 0.1, 1.9),
        "bottom_sender": normal_values(streams_of[21], (LAT, HID), LAT ** -0.5, 0.25, ((1, 2),), jnp.float32),
        "bottom_receiver": normal_values(streams_of[22], (LAT, HID), LAT ** -0.5, 0.25, ((1, 2),), jnp.float32),
        "bottom_bias": normal_values(streams_of[23], (HID,), 1.0, 4.0, ((0, 2),), jnp.float32),
        "bottom_output": normal_values(streams_of[24], (HID, LAT), HID ** -0.5, 0.25, ((0, 2),), jnp.float32),
        "bottom_gain": jnp.clip(1.0 + 0.18 * jax.random.normal(streams_of[25], (LAT,), jnp.float32), 0.1, 1.9),
    }


epsilon = 1e-05
highest = lax.Precision.HIGHEST

def project(states, weights):
    return jnp.dot(states, weights, precision=highest, preferred_element_type=jnp.float32)

def layer_norm(values):
    center = values - lax.optimization_barrier(jnp.mean(values, axis=-1, keepdims=True))
    spread = lax.optimization_barrier(jnp.mean(center * center, axis=-1, keepdims=True))
    return center * lax.rsqrt(spread + epsilon)

def interact(senders, receivers, link_index, sender_weights, receiver_weights, bias_vector, output_weights, gain_vector):
    sender_rows = project(senders, sender_weights)
    receiver_rows = project(receivers, receiver_weights) + bias_vector
    hidden = jnp.zeros_like(receiver_rows)
    for column in range(link_index.shape[1]):
        hidden = hidden + jax.nn.silu(sender_rows[link_index[:, column]] + receiver_rows)
    update = project(hidden, output_weights)
    return receivers + gain_vector * layer_norm(update)

def reference(node_states, coarse_states, children, down_sources, bottom_links, coarse_links, upward_sender, upward_receiver, upward_bias, upward_output, upward_gain, coarse_sender, coarse_receiver, coarse_bias, coarse_output, coarse_gain, downward_sender, downward_receiver, downward_bias, downward_output, downward_gain, bottom_sender, bottom_receiver, bottom_bias, bottom_output, bottom_gain):
    coarse_block = (jnp.arange(NC, dtype=jnp.int32) // CDEV)[:, None]
    child_index = (coarse_block * ROWS_DEV + children).astype(jnp.int32)
    node_block = (jnp.arange(NB, dtype=jnp.int32) // ROWS_DEV)[:, None]
    down_index = (node_block * CDEV + down_sources).astype(jnp.int32)
    mesh_index = ((node_block * ROWS_DEV + bottom_links - HALO) % NB).astype(jnp.int32)
    coarse_up = interact(node_states, coarse_states, child_index, upward_sender, upward_receiver, upward_bias, upward_output, upward_gain)
    new_coarse = interact(coarse_up, coarse_up, coarse_links, coarse_sender, coarse_receiver, coarse_bias, coarse_output, coarse_gain)
    nodes_down = interact(new_coarse, node_states, down_index, downward_sender, downward_receiver, downward_bias, downward_output, downward_gain)
    new_nodes = interact(nodes_down, nodes_down, mesh_index, bottom_sender, bottom_receiver, bottom_bias, bottom_output, bottom_gain)
    return (new_nodes, new_coarse)
```

```python
import functools

import jax
import jax.numpy as jnp
from jax import lax
from jax.experimental import pallas as pl
from jax.experimental.pallas import tpu as pltpu
from jax.sharding import PartitionSpec as P

epsilon = 1e-05
f32 = jnp.float32
bf16 = jnp.bfloat16
MESH = pl.DeviceIdType.MESH


def split(x):
    high = x.astype(bf16)
    return high, (x - high.astype(f32)).astype(bf16)


def mm(a, b):
    return jnp.dot(a, b, preferred_element_type=f32)


def dot3(x, w):
    return mm(
        jnp.concatenate([x[0], x[0], x[1]], axis=1), jnp.concatenate([w[0], w[1], w[0]], axis=0)
    )


def layer_norm(values):
    center = values - jnp.mean(values, axis=-1, keepdims=True)
    spread = jnp.mean(center * center, axis=-1, keepdims=True)
    return center * lax.rsqrt(spread + epsilon)


def pick(links, table, base):
    rows, count = links.shape[0], table[0].shape[0]
    lanes = lax.broadcasted_iota(jnp.int32, (rows, count), 1)
    hot = jnp.concatenate(
        [
            jnp.where(lanes == links[:, k : k + 1] - base, 1.0, 0.0).astype(bf16)
            for k in range(links.shape[1])
        ],
        axis=0,
    )
    return mm(jnp.concatenate([hot, hot], axis=1), jnp.concatenate(table, axis=0))


def hidden_sum(picked, receiver):
    rows = receiver.shape[0]
    total = None
    for k in range(picked.shape[0] // rows):
        h = picked[k * rows : (k + 1) * rows] + receiver
        term = h + h * jnp.tanh(h)
        total = term if total is None else total + term
    return total


def kernel(
    n_parts,
    n_patch,
    n_sub,
    n_lvl,
    rim,
    tile,
    nodes_hbm,
    coarse_hbm,
    us_hbm, ur_hbm, uo_hbm,
    cs_hbm, cr_hbm, co_hbm,
    ds_hbm, dr_hbm, do_hbm,
    bs_hbm, br_hbm, bo_hbm,
    children, down_sources, bottom_links, coarse_links,
    ub, ug, cb, cg, db, dg, bb, bg,
    out_nodes,
    out_coarse,
    ns, cs, w_in, w_mid, full_in, full_out, pair_in, pair_out, bias,
    ns_pair, rd, rb, nd, ext, near, hidden, links_out, links_in, coarse_ext,
    table, parts,
    load_sem, x_send, x_recv, y_send, y_recv, c_send, c_recv, bias_send, bias_recv,
    part_send, part_recv, tab_send, tab_recv, rel_send, rel_recv,
    node_send, node_recv, link_send, link_recv, halo_send, halo_recv,
):
    part = lax.axis_index("parts")
    patch = lax.axis_index("patch")
    sub = lax.axis_index("sub")
    lvl = lax.axis_index("lvl")
    rows = nd.shape[0] - 2 * rim
    inner = slice(rim, rim + rows)
    width = table.shape[2]
    tiles = rows // tile
    block = patch * n_lvl + lvl
    blocks = n_patch * n_lvl

    def at_part(o):
        return {"parts": lax.rem(part + o, n_parts)}

    def at_sub(o):
        return {"sub": lax.rem(sub + o, n_sub)}

    def at_lvl(o):
        return {"lvl": lax.rem(lvl + o, n_lvl)}

    def at_patch(o):
        return {"patch": lax.rem(patch + o, n_patch)}

    def at_block(o):
        other = lax.rem(block + o + blocks, blocks)
        return {"patch": other // n_lvl, "lvl": lax.rem(other, n_lvl)}

    def from_part(o):
        return lax.rem(part - o + n_parts, n_parts)

    def from_sub(o):
        return lax.rem(sub - o + n_sub, n_sub)

    def from_patch(o):
        return lax.rem(patch - o + n_patch, n_patch)

    def from_lvl(o):
        return lax.rem(lvl - o + n_lvl, n_lvl)

    def remote(src, dst, send, recv, device):
        return pltpu.make_async_remote_copy(
            src_ref=src, dst_ref=dst, send_sem=send, recv_sem=recv,
            device_id=device, device_id_type=MESH,
        )

    shared = (dr_hbm, ds_hbm, do_hbm, bs_hbm, br_hbm, bo_hbm)
    place = (
        full_in.at[0], full_in.at[1], full_out.at[0], full_in.at[2], full_in.at[3], full_out.at[1],
    )
    pairs = (
        pair_in.at[0], pair_in.at[1], pair_out.at[0], pair_in.at[2], pair_in.at[3], pair_out.at[1],
    )
    DR, DS, DO, BS, BR, BO = range(6)

    plan = [
        (us_hbm, w_in.at[0]), (nodes_hbm, ns.at[inner]), (ur_hbm, w_in.at[1]), (coarse_hbm, cs),
        (uo_hbm, w_mid.at[0]), (cs_hbm, w_in.at[2]), (cr_hbm, w_in.at[3]), (co_hbm, w_mid.at[1]),
    ]
    plan += [(shared[w], place[w].at[sub]) for w in range(6)]
    loads = [
        pltpu.make_async_copy(src, dst, load_sem.at[i]) for i, (src, dst) in enumerate(plan)
    ]
    for load in loads:
        load.start()
    l_us, l_ns, l_ur, l_cst, l_uo, l_cs, l_cr, l_co = loads[:8]
    l_own = loads[8:]

    barrier = pltpu.get_barrier_semaphore()
    peers = [at_sub(o) for o in range(1, n_sub)]
    peers += [at_part(o) for o in range(1, n_parts)]
    peers += [at_lvl(o) for o in range(1, n_lvl)]
    peers += [at_patch(o) for o in range(1, n_patch)]
    peers += [at_block(-1), at_block(1)]
    for peer in peers:
        pl.semaphore_signal(barrier, inc=1, device_id=peer, device_id_type=MESH)

    def x_copy(w, o, owner):
        size = shared[w].shape[0] // (n_lvl * n_parts)
        mine = pl.ds(pl.multiple_of((lvl * n_parts + part) * size, size), size)
        return remote(
            shared[w].at[mine], place[w].at[owner, mine],
            x_send.at[w, o - 1], x_recv.at[w, o - 1], at_sub(o),
        )

    def y_copy(w, o, q, holder):
        size = shared[w].shape[0] // (n_lvl * n_parts)
        piece = pl.ds(pl.multiple_of((lvl * n_parts + holder) * size, size), size)
        ref = place[w].at[from_sub(o), piece]
        return remote(ref, ref, y_send.at[w, o - 1, q - 1], y_recv.at[w, o - 1, q - 1], at_part(q))

    def c_copy(w, o, q, holder):
        size = shared[w].shape[0] // n_lvl
        piece = pl.ds(pl.multiple_of(holder * size, size), size)
        ref = place[w].at[from_sub(o), piece]
        return remote(ref, ref, c_send.at[w, o - 1, q - 1], c_recv.at[w, o - 1, q - 1], at_lvl(q))

    def start_x(w):
        for o in range(1, n_sub):
            x_copy(w, o, sub).start()

    def forward_y(w):
        for o in range(1, n_sub):
            x_copy(w, o, from_sub(o)).wait_recv()
            for q in range(1, n_parts):
                y_copy(w, o, q, part).start()

    def forward_c(w):
        for o in range(1, n_sub):
            for q in range(1, n_parts):
                y_copy(w, o, q, from_part(q)).wait_recv()
            for q in range(1, n_lvl):
                c_copy(w, o, q, lvl).start()

    def store_pair(w, s):
        high, low = split(place[w][s])
        pairs[w][s, 0] = high
        pairs[w][s, 1] = low

    def own(w):
        l_own[w].wait()
        store_pair(w, sub)

    def take(w):
        for o in range(1, n_sub):
            for q in range(1, n_lvl):
                c_copy(w, o, q, from_lvl(q)).wait_recv()
        for o in range(1, n_sub):
            store_pair(w, from_sub(o))

    def bias_copy(o, owner):
        return remote(
            bias.at[owner], bias.at[owner], bias_send.at[o - 1], bias_recv.at[o - 1], at_sub(o)
        )

    def part_copy(j, o, index):
        return remote(
            parts.at[j, index], parts.at[j, index],
            part_send.at[j, o - 1], part_recv.at[j, o - 1], at_sub(o),
        )

    def send_part(j):
        for o in range(1, n_sub):
            part_copy(j, o, sub).start()

    def total_part(j):
        for o in range(1, n_sub):
            part_copy(j, o, from_sub(o)).wait_recv()
        total = parts[j, 0]
        for s in range(1, n_sub):
            total = total + parts[j, s]
        return total

    l_us.wait()
    l_ns.wait()
    high, low = split(ns[inner])
    ns_pair[0, inner] = high
    ns_pair[1, inner] = low
    sender = split(0.5 * dot3((high, low), split(w_in[0])))
    l_ur.wait()
    l_cst.wait()
    receiver = 0.5 * (dot3(split(cs[...]), split(w_in[1])) + ub[...])
    hid = hidden_sum(pick(jnp.transpose(children[...]), sender, 0), receiver)
    l_uo.wait()
    parts[0, sub] = dot3(split(hid), split(w_mid[0]))
    bias[sub, 0:1] = db[...]
    bias[sub, 1:2] = bb[...]

    links_out[...] = jnp.zeros_like(links_out)
    links_out[: down_sources.shape[0]] = down_sources[...]

    def node_copy(side):
        source = slice(0, rim) if side == 0 else slice(rows - rim, rows)
        target = slice(rim + rows, rows + 2 * rim) if side == 0 else slice(0, rim)
        return remote(
            nodes_hbm.at[source], ns.at[target], node_send.at[side], node_recv.at[side],
            at_block(2 * side - 1),
        )

    def link_copy(side):
        source = slice(0, rim) if side == 0 else slice(rows - rim, rows)
        return remote(
            links_out.at[:, source], links_in.at[1 - side], link_send.at[side],
            link_recv.at[side], at_block(2 * side - 1),
        )

    def halo_copy(side):
        return remote(
            coarse_ext.at[1], coarse_ext.at[2 - 2 * side], halo_send.at[side], halo_recv.at[side],
            at_block(2 * side - 1),
        )

    pl.semaphore_wait(barrier, len(peers))
    send_part(0)
    for o in range(1, n_sub):
        bias_copy(o, sub).start()
    for side in range(2):
        node_copy(side).start()
        link_copy(side).start()
    start_x(DR)
    start_x(DS)

    def receive_down(s, piece):
        value = dot3(
            (ns_pair[0, piece], ns_pair[1, piece]), (pair_in[0, s, 0], pair_in[0, s, 1])
        )
        rd[s, piece] = 0.5 * (value + bias[s, 0:1])

    own(DR)
    receive_down(sub, inner)
    near[:, : bottom_links.shape[0]] = jnp.transpose(bottom_links[...])
    l_cs.wait()
    l_cr.wait()
    w_send = split(w_in[2])
    coarse_up = cs[...] + ug[...] * layer_norm(total_part(0))

    up_pair = split(coarse_up)
    table[block] = 0.5 * dot3(up_pair, w_send)

    def tab_copy(o, index):
        return remote(
            table.at[index], table.at[index], tab_send.at[o - 1], tab_recv.at[o - 1], at_patch(o)
        )

    def rel_copy(o, q, index):
        return remote(
            table.at[index], table.at[index],
            rel_send.at[o, q - 1], rel_recv.at[o, q - 1], at_lvl(q),
        )

    order = sorted(range(1, n_patch), key=lambda o: min(o, n_patch - o))
    for o in order:
        tab_copy(o, block).start()
    for q in range(1, n_lvl):
        rel_copy(0, q, block).start()
    receiver = 0.5 * (dot3(up_pair, split(w_in[3])) + cb[...])
    for w in (DS, DO, BS, BR, BO):
        own(w)
    forward_y(DR)
    start_x(DO)
    outer = (slice(0, rim), slice(rim + rows, rows + 2 * rim))
    for side in range(2):
        node_copy(1 - side).wait_recv()
        link_copy(1 - side).wait_recv()
        high, low = split(ns[outer[side]])
        ns_pair[0, outer[side]] = high
        ns_pair[1, outer[side]] = low
        receive_down(sub, outer[side])
    for o in range(1, n_sub):
        bias_copy(o, from_sub(o)).wait_recv()
    forward_y(DS)
    start_x(BS)
    forward_c(DR)
    for o in order:
        tab_copy(o, from_patch(o) * n_lvl + lvl).wait_recv()
        for q in range(1, n_lvl):
            rel_copy(o, q, from_patch(o) * n_lvl + lvl).start()
    for q in range(1, n_lvl):
        rel_copy(0, q, patch * n_lvl + from_lvl(q)).wait_recv()
    for o in order:
        for q in range(1, n_lvl):
            rel_copy(o, q, from_patch(o) * n_lvl + from_lvl(q)).wait_recv()

    cells = table.shape[1]
    chunk = max(d for d in range(1, blocks + 1) if blocks % d == 0 and d * cells <= 512)
    coarse_columns = jnp.transpose(coarse_links[...])
    picked = None
    for c in range(0, blocks, chunk):
        rows_pair = split(table[c : c + chunk].reshape(chunk * cells, width))
        got = pick(coarse_columns, rows_pair, c * cells)
        picked = got if picked is None else picked + got
    hid = hidden_sum(picked, receiver)
    l_co.wait()
    parts[1, sub] = dot3(split(hid), split(w_mid[1]))
    send_part(1)
    forward_y(DO)
    start_x(BR)
    forward_c(DS)
    take(DR)
    for o in range(1, n_sub):
        receive_down(from_sub(o), slice(None))
    take(DS)
    forward_c(DO)
    take(DO)
    new_coarse = coarse_up + cg[...] * layer_norm(total_part(1))
    coarse_ext[1] = new_coarse
    for side in range(2):
        halo_copy(side).start()
    out_coarse[...] = new_coarse
    forward_y(BS)
    start_x(BO)

    def whole(ref, k, axis):
        return jnp.concatenate([ref[s, k] for s in range(n_sub)], axis=axis)

    down_columns = (
        jnp.transpose(links_in[0]), jnp.transpose(links_out[...]), jnp.transpose(links_in[1]),
    )
    lanes = lax.rem(lax.broadcasted_iota(jnp.int32, (tile, 2 * cells), 1), cells)

    def down_table(i):
        w_send = (whole(pair_in.at[1], 0, 1), whole(pair_in.at[1], 1, 1))
        return jnp.concatenate(split(0.5 * dot3(split(coarse_ext[i]), w_send)), axis=0)

    def descend(t, columns, rows_pair):
        piece = slice(t * tile, (t + 1) * tile)
        hot = jnp.concatenate(
            [
                jnp.where(lanes == columns[:, k : k + 1], 1.0, 0.0).astype(bf16)
                for k in range(down_sources.shape[0])
            ],
            axis=0,
        )
        receiver = jnp.concatenate([rd[s, piece] for s in range(n_sub)], axis=1)
        hid = hidden_sum(mm(hot, rows_pair), receiver)
        w_out = (whole(pair_out.at[0], 0, 0), whole(pair_out.at[0], 1, 0))
        nd[piece] = ns[piece] + dg[...] * layer_norm(dot3(split(hid), w_out))

    def project(t):
        piece = slice(t * tile, (t + 1) * tile)
        w_send = (whole(pair_in.at[2], 0, 1), whole(pair_in.at[2], 1, 1))
        high, low = split(0.5 * dot3(split(nd[piece]), w_send))
        ext[0, piece] = high
        ext[1, piece] = low

    def receive_bottom(t):
        piece = slice((t + 1) * tile, (t + 2) * tile)
        w_receive = (whole(pair_in.at[3], 0, 1), whole(pair_in.at[3], 1, 1))
        both = jnp.concatenate([bias[s, 1:2] for s in range(n_sub)], axis=1)
        rb[t * tile : (t + 1) * tile] = 0.5 * (dot3(split(nd[piece]), w_receive) + both)

    def bottom(t):
        piece = slice(t * tile, (t + 1) * tile)
        window = slice(t * tile, (t + 1) * tile + 2 * rim)
        picked = pick(
            near[piece, : bottom_links.shape[0]], (ext[0, window], ext[1, window]), t * tile
        )
        hidden[piece] = hidden_sum(picked, rb[piece])

    def finish(t):
        piece = slice(t * tile, (t + 1) * tile)
        w_out = (whole(pair_out.at[1], 0, 0), whole(pair_out.at[1], 1, 0))
        update = layer_norm(dot3(split(hidden[piece]), w_out))
        out_nodes[piece] = nd[(t + 1) * tile : (t + 2) * tile] + bg[...] * update

    rows_pair = down_table(1)
    for t in range(tiles):
        descend(t + 1, down_columns[1][t * tile : (t + 1) * tile], rows_pair)
    forward_y(BR)
    forward_c(BS)
    for side in range(2):
        halo_copy(1 - side).wait_recv()
        descend(side * (tiles + 1), down_columns[2 * side], down_table(2 * side))
    take(BS)
    for t in range(tiles + 2):
        project(t)
    forward_y(BO)
    forward_c(BR)
    take(BR)
    for t in range(tiles):
        receive_bottom(t)
    for t in range(tiles):
        bottom(t)
    forward_c(BO)
    take(BO)
    for t in range(tiles):
        finish(t)

    for o in range(1, n_sub):
        for w in range(6):
            x_copy(w, o, sub).wait_send()
            for q in range(1, n_parts):
                y_copy(w, o, q, part).wait_send()
            for q in range(1, n_lvl):
                c_copy(w, o, q, lvl).wait_send()
        bias_copy(o, sub).wait_send()
        for j in range(2):
            part_copy(j, o, sub).wait_send()
    for o in order:
        tab_copy(o, block).wait_send()
        for q in range(1, n_lvl):
            rel_copy(o, q, from_patch(o) * n_lvl + lvl).wait_send()
    for q in range(1, n_lvl):
        rel_copy(0, q, block).wait_send()
    for side in range(2):
        node_copy(side).wait_send()
        link_copy(side).wait_send()
        halo_copy(side).wait_send()


def body(
    node_states, coarse_states, children, down_sources, bottom_links, coarse_links,
    upward_sender, upward_receiver, upward_bias, upward_output, upward_gain,
    coarse_sender, coarse_receiver, coarse_bias, coarse_output, coarse_gain,
    downward_sender, downward_receiver, downward_bias, downward_output, downward_gain,
    bottom_sender, bottom_receiver, bottom_bias, bottom_output, bottom_gain,
):
    n_parts, n_patch, n_sub, n_lvl = (
        lax.axis_size(a) for a in ("parts", "patch", "sub", "lvl")
    )
    rows, lat = node_states.shape
    cells = coarse_states.shape[0]
    width = upward_sender.shape[1]
    hid = width * n_sub
    rim = rows // 4
    tile = rim
    blocks = n_patch * n_lvl
    subs, others, cores = max(n_sub - 1, 1), max(n_parts - 1, 1), max(n_lvl - 1, 1)
    row = lambda v: v.reshape(1, -1)
    dma = pltpu.SemaphoreType.DMA
    vmem = pl.BlockSpec(memory_space=pltpu.VMEM)
    anywhere = pl.BlockSpec(memory_space=pl.ANY)
    return pl.pallas_call(
        functools.partial(kernel, n_parts, n_patch, n_sub, n_lvl, rim, tile),
        out_shape=(
            jax.ShapeDtypeStruct((rows, lat), f32),
            jax.ShapeDtypeStruct((cells, lat), f32),
        ),
        in_specs=[anywhere] * 14 + [vmem] * 12,
        out_specs=(vmem, vmem),
        scratch_shapes=[
            pltpu.VMEM((rows + 2 * rim, lat), f32),
            pltpu.VMEM((cells, lat), f32),
            pltpu.VMEM((4, lat, width), f32),
            pltpu.VMEM((2, width, lat), f32),
            pltpu.VMEM((4, n_sub, lat, width), f32),
            pltpu.VMEM((2, n_sub, width, lat), f32),
            pltpu.VMEM((4, n_sub, 2, lat, width), bf16),
            pltpu.VMEM((2, n_sub, 2, width, lat), bf16),
            pltpu.VMEM((n_sub, 8, width), f32),
            pltpu.VMEM((2, rows + 2 * rim, lat), bf16),
            pltpu.VMEM((n_sub, rows + 2 * rim, width), f32),
            pltpu.VMEM((rows, hid), f32),
            pltpu.VMEM((rows + 2 * rim, lat), f32),
            pltpu.VMEM((2, rows + 2 * rim, hid), bf16),
            pltpu.VMEM((rows, 128), jnp.int32),
            pltpu.VMEM((rows, hid), f32),
            pltpu.VMEM((8, rows), jnp.int32),
            pltpu.VMEM((2, 8, rim), jnp.int32),
            pltpu.VMEM((3, cells, lat), f32),
            pltpu.VMEM((blocks, cells, width), f32),
            pltpu.VMEM((2, n_sub, cells, lat), f32),
            dma((14,)),
            dma((6, subs)),
            dma((6, subs)),
            dma((6, subs, others)),
            dma((6, subs, others)),
            dma((6, subs, cores)),
            dma((6, subs, cores)),
            dma((subs,)),
            dma((subs,)),
            dma((2, subs)),
            dma((2, subs)),
            dma((n_patch,)),
            dma((n_patch,)),
            dma((n_patch, cores)),
            dma((n_patch, cores)),
            dma((2,)),
            dma((2,)),
            dma((2,)),
            dma((2,)),
            dma((2,)),
            dma((2,)),
        ],
        compiler_params=pltpu.CompilerParams(
            collective_id=0, has_side_effects=True, vmem_limit_bytes=60 * 1024 * 1024
        ),
        name="sweep",
    )(
        node_states, coarse_states,
        upward_sender, upward_receiver, upward_output,
        coarse_sender, coarse_receiver, coarse_output,
        downward_sender, downward_receiver, downward_output,
        bottom_sender, bottom_receiver, bottom_output,
        children.T, down_sources.T, bottom_links.T, coarse_links.T,
        row(upward_bias), row(upward_gain), row(coarse_bias), row(coarse_gain),
        row(downward_bias), row(downward_gain), row(bottom_bias), row(bottom_gain),
    )


def solution(mesh):
    rows = P(("parts", "patch", "lvl"), None)
    links = P(("patch", "lvl"), None)
    weights = (P(None, "sub"), P(None, "sub"), P("sub"), P("sub", None), P())
    in_specs = (rows, rows, links, links, links, links) + weights * 4
    return jax.shard_map(
        body, mesh=mesh, in_specs=in_specs, out_specs=(rows, rows), check_vma=False
    )
```

```python
import functools

import jax
import jax.numpy as jnp
from jax import lax
from jax.experimental import pallas as pl
from jax.experimental.pallas import tpu as pltpu
from jax.sharding import PartitionSpec as P

epsilon = 1e-05
f32 = jnp.float32
bf16 = jnp.bfloat16
MESH = pl.DeviceIdType.MESH


def split(x):
    high = x.astype(bf16)
    return high, (x - high.astype(f32)).astype(bf16)


def mm(a, b):
    return jnp.dot(a, b, preferred_element_type=f32)


def dot3(x, w):
    return mm(
        jnp.concatenate([x[0], x[0], x[1]], axis=1), jnp.concatenate([w[0], w[1], w[0]], axis=0)
    )


def layer_norm(values):
    center = values - jnp.mean(values, axis=-1, keepdims=True)
    spread = jnp.mean(center * center, axis=-1, keepdims=True)
    return center * lax.rsqrt(spread + epsilon)


def pick(links, table, base):
    rows, count = links.shape[0], table[0].shape[0]
    lanes = lax.broadcasted_iota(jnp.int32, (rows, count), 1)
    hot = jnp.concatenate(
        [
            jnp.where(lanes == links[:, k : k + 1] - base, 1.0, 0.0).astype(bf16)
            for k in range(links.shape[1])
        ],
        axis=0,
    )
    return mm(jnp.concatenate([hot, hot], axis=1), jnp.concatenate(table, axis=0))


def hidden_sum(picked, receiver):
    rows = receiver.shape[0]
    total = None
    for k in range(picked.shape[0] // rows):
        h = picked[k * rows : (k + 1) * rows] + receiver
        term = h + h * jnp.tanh(h)
        total = term if total is None else total + term
    return total


def kernel(
    n_parts,
    n_patch,
    n_sub,
    n_lvl,
    rim,
    tile,
    nodes_hbm,
    coarse_hbm,
    us_hbm, ur_hbm, uo_hbm,
    cs_hbm, cr_hbm, co_hbm,
    ds_hbm, dr_hbm, do_hbm,
    bs_hbm, br_hbm, bo_hbm,
    children, down_sources, bottom_links, coarse_links,
    ub, ug, cb, cg, db, dg, bb, bg,
    out_nodes,
    out_coarse,
    ns, cs, w_in, w_mid, full_in, full_out, pair_in, pair_out, bias,
    ns_pair, rd, rb, nd, ext, near, hidden, links_out, links_in, coarse_ext,
    table, parts,
    load_sem, x_send, x_recv, y_send, y_recv, c_send, c_recv, bias_send, bias_recv,
    part_send, part_recv, tab_send, tab_recv, rel_send, rel_recv,
    node_send, node_recv, link_send, link_recv, halo_send, halo_recv,
):
    part = lax.axis_index("parts")
    patch = lax.axis_index("patch")
    sub = lax.axis_index("sub")
    lvl = lax.axis_index("lvl")
    rows = nd.shape[0] - 2 * rim
    inner = slice(rim, rim + rows)
    width = table.shape[2]
    tiles = rows // tile
    block = patch * n_lvl + lvl
    blocks = n_patch * n_lvl

    def at_part(o):
        return {"parts": lax.rem(part + o, n_parts)}

    def at_sub(o):
        return {"sub": lax.rem(sub + o, n_sub)}

    def at_lvl(o):
        return {"lvl": lax.rem(lvl + o, n_lvl)}

    def at_patch(o):
        return {"patch": lax.rem(patch + o, n_patch)}

    def at_block(o):
        other = lax.rem(block + o + blocks, blocks)
        return {"patch": other // n_lvl, "lvl": lax.rem(other, n_lvl)}

    pairing = 2 if n_patch % 2 == 0 else 1
    in_pair = lax.rem(patch, pairing)
    group = [(p, z) for z in range(pairing) for p in range(n_parts) if p or z]

    def at_group(d):
        other = patch + 1 - 2 * in_pair if d[1] else patch
        return {"parts": lax.rem(part + d[0], n_parts), "patch": other}

    def from_group(d):
        other = 1 - in_pair if d[1] else in_pair
        return lax.rem(part - d[0] + n_parts, n_parts), other

    def from_sub(o):
        return lax.rem(sub - o + n_sub, n_sub)

    def from_patch(o):
        return lax.rem(patch - o + n_patch, n_patch)

    def from_lvl(o):
        return lax.rem(lvl - o + n_lvl, n_lvl)

    def remote(src, dst, send, recv, device):
        return pltpu.make_async_remote_copy(
            src_ref=src, dst_ref=dst, send_sem=send, recv_sem=recv,
            device_id=device, device_id_type=MESH,
        )

    shared = (dr_hbm, ds_hbm, do_hbm, bs_hbm, br_hbm, bo_hbm)
    place = (
        full_in.at[0], full_in.at[1], full_out.at[0], full_in.at[2], full_in.at[3], full_out.at[1],
    )
    pairs = (
        pair_in.at[0], pair_in.at[1], pair_out.at[0], pair_in.at[2], pair_in.at[3], pair_out.at[1],
    )
    DR, DS, DO, BS, BR, BO = range(6)
    paired = (BS, BR, BO)

    plan = [
        (us_hbm, w_in.at[0]), (nodes_hbm, ns.at[inner]), (ur_hbm, w_in.at[1]), (coarse_hbm, cs),
        (uo_hbm, w_mid.at[0]), (cs_hbm, w_in.at[2]), (cr_hbm, w_in.at[3]), (co_hbm, w_mid.at[1]),
    ]
    plan += [(shared[w], place[w].at[sub]) for w in range(6)]
    loads = [
        pltpu.make_async_copy(src, dst, load_sem.at[i]) for i, (src, dst) in enumerate(plan)
    ]
    for load in loads:
        load.start()
    l_us, l_ns, l_ur, l_cst, l_uo, l_cs, l_cr, l_co = loads[:8]
    l_own = loads[8:]

    barrier = pltpu.get_barrier_semaphore()
    peers = [at_sub(o) for o in range(1, n_sub)]
    peers += [at_part(o) for o in range(1, n_parts)]
    peers += [at_lvl(o) for o in range(1, n_lvl)]
    peers += [at_patch(o) for o in range(1, n_patch)]
    peers += [at_block(-1), at_block(1)]
    peers += [at_group(d) for d in group[n_parts - 1 :] if d[0]]
    for peer in peers:
        pl.semaphore_signal(barrier, inc=1, device_id=peer, device_id_type=MESH)

    def piece_of(w, core, holder):
        side, pair = holder
        count = n_parts * pairing if w in paired else n_parts
        index = core * count + (side * pairing + pair if w in paired else side)
        size = shared[w].shape[0] // (n_lvl * count)
        return pl.ds(pl.multiple_of(index * size, size), size)

    def x_copy(w, o, owner):
        mine = piece_of(w, lvl, (part, in_pair))
        return remote(
            shared[w].at[mine], place[w].at[owner, mine],
            x_send.at[w, o - 1], x_recv.at[w, o - 1], at_sub(o),
        )

    def y_copy(w, o, q, holder):
        ref = place[w].at[from_sub(o), piece_of(w, lvl, holder)]
        return remote(
            ref, ref, y_send.at[w, o - 1, q], y_recv.at[w, o - 1, q], at_group(group[q])
        )

    def ways(w):
        return range(len(group) if w in paired else n_parts - 1)

    def c_copy(w, o, q, holder):
        size = shared[w].shape[0] // n_lvl
        piece = pl.ds(pl.multiple_of(holder * size, size), size)
        ref = place[w].at[from_sub(o), piece]
        return remote(ref, ref, c_send.at[w, o - 1, q - 1], c_recv.at[w, o - 1, q - 1], at_lvl(q))

    def start_x(w):
        for o in range(1, n_sub):
            x_copy(w, o, sub).start()

    def forward_y(w):
        for o in range(1, n_sub):
            x_copy(w, o, from_sub(o)).wait_recv()
            for q in ways(w):
                y_copy(w, o, q, (part, in_pair)).start()

    def forward_c(w):
        for o in range(1, n_sub):
            for q in ways(w):
                y_copy(w, o, q, from_group(group[q])).wait_recv()
            for q in range(1, n_lvl):
                c_copy(w, o, q, lvl).start()

    def store_pair(w, s):
        high, low = split(place[w][s])
        pairs[w][s, 0] = high
        pairs[w][s, 1] = low

    def own(w):
        l_own[w].wait()
        store_pair(w, sub)

    def take(w):
        for o in range(1, n_sub):
            for q in range(1, n_lvl):
                c_copy(w, o, q, from_lvl(q)).wait_recv()
        for o in range(1, n_sub):
            store_pair(w, from_sub(o))

    def bias_copy(o, owner):
        return remote(
            bias.at[owner], bias.at[owner], bias_send.at[o - 1], bias_recv.at[o - 1], at_sub(o)
        )

    def part_copy(j, o, index):
        return remote(
            parts.at[j, index], parts.at[j, index],
            part_send.at[j, o - 1], part_recv.at[j, o - 1], at_sub(o),
        )

    def send_part(j):
        for o in range(1, n_sub):
            part_copy(j, o, sub).start()

    def total_part(j):
        for o in range(1, n_sub):
            part_copy(j, o, from_sub(o)).wait_recv()
        total = parts[j, 0]
        for s in range(1, n_sub):
            total = total + parts[j, s]
        return total

    l_us.wait()
    l_ns.wait()
    high, low = split(ns[inner])
    ns_pair[0, inner] = high
    ns_pair[1, inner] = low
    sender = split(0.5 * dot3((high, low), split(w_in[0])))
    l_ur.wait()
    l_cst.wait()
    receiver = 0.5 * (dot3(split(cs[...]), split(w_in[1])) + ub[...])
    hid = hidden_sum(pick(jnp.transpose(children[...]), sender, 0), receiver)
    l_uo.wait()
    parts[0, sub] = dot3(split(hid), split(w_mid[0]))
    bias[sub, 0:1] = db[...]
    bias[sub, 1:2] = bb[...]

    links_out[...] = jnp.zeros_like(links_out)
    links_out[: down_sources.shape[0]] = down_sources[...]

    def node_copy(side):
        source = slice(0, rim) if side == 0 else slice(rows - rim, rows)
        target = slice(rim + rows, rows + 2 * rim) if side == 0 else slice(0, rim)
        return remote(
            nodes_hbm.at[source], ns.at[target], node_send.at[side], node_recv.at[side],
            at_block(2 * side - 1),
        )

    def link_copy(side):
        source = slice(0, rim) if side == 0 else slice(rows - rim, rows)
        return remote(
            links_out.at[:, source], links_in.at[1 - side], link_send.at[side],
            link_recv.at[side], at_block(2 * side - 1),
        )

    def halo_copy(side):
        return remote(
            coarse_ext.at[1], coarse_ext.at[2 - 2 * side], halo_send.at[side], halo_recv.at[side],
            at_block(2 * side - 1),
        )

    pl.semaphore_wait(barrier, len(peers))
    send_part(0)
    for o in range(1, n_sub):
        bias_copy(o, sub).start()
    for side in range(2):
        link_copy(side).start()
    node_copy(0).start()
    start_x(DR)
    start_x(DS)

    def receive_down(s, piece):
        value = dot3(
            (ns_pair[0, piece], ns_pair[1, piece]), (pair_in[0, s, 0], pair_in[0, s, 1])
        )
        rd[s, piece] = 0.5 * (value + bias[s, 0:1])

    own(DR)
    receive_down(sub, inner)
    near[:, : bottom_links.shape[0]] = jnp.transpose(bottom_links[...])
    l_cs.wait()
    l_cr.wait()
    w_send = split(w_in[2])
    coarse_up = cs[...] + ug[...] * layer_norm(total_part(0))

    up_pair = split(coarse_up)
    table[block] = 0.5 * dot3(up_pair, w_send)

    def tab_copy(o, index):
        return remote(
            table.at[index], table.at[index], tab_send.at[o - 1], tab_recv.at[o - 1], at_patch(o)
        )

    def rel_copy(o, q, index):
        return remote(
            table.at[index], table.at[index],
            rel_send.at[o, q - 1], rel_recv.at[o, q - 1], at_lvl(q),
        )

    order = sorted(range(1, n_patch), key=lambda o: min(o, n_patch - o))
    for o in order:
        tab_copy(o, block).start()
    for q in range(1, n_lvl):
        rel_copy(0, q, block).start()
    receiver = 0.5 * (dot3(up_pair, split(w_in[3])) + cb[...])
    for w in (DS, DO, BS, BR, BO):
        own(w)
    forward_y(DR)
    start_x(DO)
    outer = (slice(0, rim), slice(rim + rows, rows + 2 * rim))

    def take_nodes(side):
        node_copy(1 - side).wait_recv()
        link_copy(1 - side).wait_recv()
        high, low = split(ns[outer[side]])
        ns_pair[0, outer[side]] = high
        ns_pair[1, outer[side]] = low
        receive_down(sub, outer[side])

    take_nodes(1)
    for o in range(1, n_sub):
        bias_copy(o, from_sub(o)).wait_recv()
    forward_y(DS)
    start_x(BS)
    for o in order:
        tab_copy(o, from_patch(o) * n_lvl + lvl).wait_recv()
        for q in range(1, n_lvl):
            rel_copy(o, q, from_patch(o) * n_lvl + lvl).start()
    for q in range(1, n_lvl):
        rel_copy(0, q, patch * n_lvl + from_lvl(q)).wait_recv()
    for o in order:
        for q in range(1, n_lvl):
            rel_copy(o, q, from_patch(o) * n_lvl + from_lvl(q)).wait_recv()

    node_copy(1).start()
    start_x(BR)
    cells = table.shape[1]
    chunk = max(d for d in range(1, blocks + 1) if blocks % d == 0 and d * cells <= 512)
    coarse_columns = jnp.transpose(coarse_links[...])
    picked = None
    for c in range(0, blocks, chunk):
        rows_pair = split(table[c : c + chunk].reshape(chunk * cells, width))
        got = pick(coarse_columns, rows_pair, c * cells)
        picked = got if picked is None else picked + got
    hid = hidden_sum(picked, receiver)
    l_co.wait()
    parts[1, sub] = dot3(split(hid), split(w_mid[1]))
    send_part(1)
    forward_c(DR)
    forward_y(DO)
    forward_y(BS)
    start_x(BO)
    forward_c(DS)
    take(DR)
    for o in range(1, n_sub):
        receive_down(from_sub(o), inner)
        receive_down(from_sub(o), outer[1])
    take(DS)
    forward_y(BR)
    new_coarse = coarse_up + cg[...] * layer_norm(total_part(1))
    coarse_ext[1] = new_coarse
    for side in range(2):
        halo_copy(side).start()
    out_coarse[...] = new_coarse
    forward_c(DO)
    forward_c(BS)
    take(DO)

    def whole(ref, k, axis):
        return jnp.concatenate([ref[s, k] for s in range(n_sub)], axis=axis)

    down_columns = jnp.transpose(links_out[...])
    lanes = lax.rem(lax.broadcasted_iota(jnp.int32, (tile, 2 * cells), 1), cells)

    def down_table(i):
        w_send = (whole(pair_in.at[1], 0, 1), whole(pair_in.at[1], 1, 1))
        return jnp.concatenate(split(0.5 * dot3(split(coarse_ext[i]), w_send)), axis=0)

    def descend(t, columns, rows_pair):
        piece = slice(t * tile, (t + 1) * tile)
        hot = jnp.concatenate(
            [
                jnp.where(lanes == columns[:, k : k + 1], 1.0, 0.0).astype(bf16)
                for k in range(down_sources.shape[0])
            ],
            axis=0,
        )
        receiver = jnp.concatenate([rd[s, piece] for s in range(n_sub)], axis=1)
        hid = hidden_sum(mm(hot, rows_pair), receiver)
        w_out = (whole(pair_out.at[0], 0, 0), whole(pair_out.at[0], 1, 0))
        nd[piece] = ns[piece] + dg[...] * layer_norm(dot3(split(hid), w_out))

    def project(t):
        piece = slice(t * tile, (t + 1) * tile)
        w_send = (whole(pair_in.at[2], 0, 1), whole(pair_in.at[2], 1, 1))
        high, low = split(0.5 * dot3(split(nd[piece]), w_send))
        ext[0, piece] = high
        ext[1, piece] = low

    def receive_bottom(t):
        piece = slice((t + 1) * tile, (t + 2) * tile)
        w_receive = (whole(pair_in.at[3], 0, 1), whole(pair_in.at[3], 1, 1))
        both = jnp.concatenate([bias[s, 1:2] for s in range(n_sub)], axis=1)
        rb[t * tile : (t + 1) * tile] = 0.5 * (dot3(split(nd[piece]), w_receive) + both)

    def bottom(t):
        piece = slice(t * tile, (t + 1) * tile)
        window = slice(t * tile, (t + 1) * tile + 2 * rim)
        picked = pick(
            near[piece, : bottom_links.shape[0]], (ext[0, window], ext[1, window]), t * tile
        )
        hidden[piece] = hidden_sum(picked, rb[piece])

    def finish(t):
        piece = slice(t * tile, (t + 1) * tile)
        w_out = (whole(pair_out.at[1], 0, 0), whole(pair_out.at[1], 1, 0))
        update = layer_norm(dot3(split(hidden[piece]), w_out))
        out_nodes[piece] = nd[(t + 1) * tile : (t + 2) * tile] + bg[...] * update

    rows_pair = down_table(1)
    for t in range(tiles):
        descend(t + 1, down_columns[t * tile : (t + 1) * tile], rows_pair)
    take_nodes(0)
    for o in range(1, n_sub):
        receive_down(from_sub(o), outer[0])
    forward_y(BO)
    take(BS)
    for t in range(tiles):
        project(t + 1)
    for side in range(2):
        halo_copy(1 - side).wait_recv()
        end = side * (tiles + 1)
        descend(end, jnp.transpose(links_in[side]), down_table(2 * side))
        project(end)
    forward_c(BR)
    take(BR)
    for t in range(tiles):
        receive_bottom(t)
    for i, t in enumerate(list(range(1, tiles - 1)) + [0, tiles - 1]):
        bottom(t)
        if i == 0:
            forward_c(BO)
    take(BO)
    for t in range(tiles):
        finish(t)

    for o in range(1, n_sub):
        for w in range(6):
            x_copy(w, o, sub).wait_send()
            for q in ways(w):
                y_copy(w, o, q, (part, in_pair)).wait_send()
            for q in range(1, n_lvl):
                c_copy(w, o, q, lvl).wait_send()
        bias_copy(o, sub).wait_send()
        for j in range(2):
            part_copy(j, o, sub).wait_send()
    for o in order:
        tab_copy(o, block).wait_send()
        for q in range(1, n_lvl):
            rel_copy(o, q, from_patch(o) * n_lvl + lvl).wait_send()
    for q in range(1, n_lvl):
        rel_copy(0, q, block).wait_send()
    for side in range(2):
        node_copy(side).wait_send()
        link_copy(side).wait_send()
        halo_copy(side).wait_send()


def hand_over(nodes, coarse, out_nodes, out_coarse):
    out_nodes[...] = nodes[...]
    out_coarse[...] = coarse[...]


def body(
    node_states, coarse_states, children, down_sources, bottom_links, coarse_links,
    upward_sender, upward_receiver, upward_bias, upward_output, upward_gain,
    coarse_sender, coarse_receiver, coarse_bias, coarse_output, coarse_gain,
    downward_sender, downward_receiver, downward_bias, downward_output, downward_gain,
    bottom_sender, bottom_receiver, bottom_bias, bottom_output, bottom_gain,
):
    n_parts, n_patch, n_sub, n_lvl = (
        lax.axis_size(a) for a in ("parts", "patch", "sub", "lvl")
    )
    rows, lat = node_states.shape
    cells = coarse_states.shape[0]
    width = upward_sender.shape[1]
    hid = width * n_sub
    rim = rows // 4
    tile = rim
    blocks = n_patch * n_lvl
    subs, others, cores = max(n_sub - 1, 1), max(2 * n_parts - 1, 1), max(n_lvl - 1, 1)
    row = lambda v: v.reshape(1, -1)
    dma = pltpu.SemaphoreType.DMA
    vmem = pl.BlockSpec(memory_space=pltpu.VMEM)
    anywhere = pl.BlockSpec(memory_space=pl.ANY)
    swept = pl.pallas_call(
        functools.partial(kernel, n_parts, n_patch, n_sub, n_lvl, rim, tile),
        out_shape=(
            jax.ShapeDtypeStruct((rows, lat), f32),
            jax.ShapeDtypeStruct((cells, lat), f32),
        ),
        in_specs=[anywhere] * 14 + [vmem] * 12,
        out_specs=(vmem, vmem),
        scratch_shapes=[
            pltpu.VMEM((rows + 2 * rim, lat), f32),
            pltpu.VMEM((cells, lat), f32),
            pltpu.VMEM((4, lat, width), f32),
            pltpu.VMEM((2, width, lat), f32),
            pltpu.VMEM((4, n_sub, lat, width), f32),
            pltpu.VMEM((2, n_sub, width, lat), f32),
            pltpu.VMEM((4, n_sub, 2, lat, width), bf16),
            pltpu.VMEM((2, n_sub, 2, width, lat), bf16),
            pltpu.VMEM((n_sub, 8, width), f32),
            pltpu.VMEM((2, rows + 2 * rim, lat), bf16),
            pltpu.VMEM((n_sub, rows + 2 * rim, width), f32),
            pltpu.VMEM((rows, hid), f32),
            pltpu.VMEM((rows + 2 * rim, lat), f32),
            pltpu.VMEM((2, rows + 2 * rim, hid), bf16),
            pltpu.VMEM((rows, 128), jnp.int32),
            pltpu.VMEM((rows, hid), f32),
            pltpu.VMEM((8, rows), jnp.int32),
            pltpu.VMEM((2, 8, rim), jnp.int32),
            pltpu.VMEM((3, cells, lat), f32),
            pltpu.VMEM((blocks, cells, width), f32),
            pltpu.VMEM((2, n_sub, cells, lat), f32),
            dma((14,)),
            dma((6, subs)),
            dma((6, subs)),
            dma((6, subs, others)),
            dma((6, subs, others)),
            dma((6, subs, cores)),
            dma((6, subs, cores)),
            dma((subs,)),
            dma((subs,)),
            dma((2, subs)),
            dma((2, subs)),
            dma((n_patch,)),
            dma((n_patch,)),
            dma((n_patch, cores)),
            dma((n_patch, cores)),
            dma((2,)),
            dma((2,)),
            dma((2,)),
            dma((2,)),
            dma((2,)),
            dma((2,)),
        ],
        compiler_params=pltpu.CompilerParams(
            collective_id=0, has_side_effects=True, vmem_limit_bytes=60 * 1024 * 1024
        ),
        name="sweep",
    )(
        node_states, coarse_states,
        upward_sender, upward_receiver, upward_output,
        coarse_sender, coarse_receiver, coarse_output,
        downward_sender, downward_receiver, downward_output,
        bottom_sender, bottom_receiver, bottom_output,
        children.T, down_sources.T, bottom_links.T, coarse_links.T,
        row(upward_bias), row(upward_gain), row(coarse_bias), row(coarse_gain),
        row(downward_bias), row(downward_gain), row(bottom_bias), row(bottom_gain),
    )
    steps = 2
    specs = [pl.BlockSpec((n // steps, lat), lambda i: (i, 0)) for n in (rows, cells)]
    return pl.pallas_call(
        hand_over,
        grid=(steps,),
        out_shape=tuple(jax.ShapeDtypeStruct(v.shape, v.dtype) for v in swept),
        in_specs=specs,
        out_specs=tuple(specs),
        name="hand_over",
    )(*swept)


def solution(mesh):
    rows = P(("parts", "patch", "lvl"), None)
    links = P(("patch", "lvl"), None)
    weights = (P(None, "sub"), P(None, "sub"), P("sub"), P("sub", None), P())
    in_specs = (rows, rows, links, links, links, links) + weights * 4
    return jax.shard_map(
        body, mesh=mesh, in_specs=in_specs, out_specs=(rows, rows), check_vma=False
    )
```

```python
import functools

import jax
import jax.numpy as jnp
from jax import lax
from jax.experimental import pallas as pl
from jax.experimental.pallas import tpu as pltpu
from jax.sharding import PartitionSpec as P

epsilon = 1e-05
f32 = jnp.float32
bf16 = jnp.bfloat16
MESH = pl.DeviceIdType.MESH


def split(x):
    high = x.astype(bf16)
    return high, (x - high.astype(f32)).astype(bf16)


def mm(a, b):
    return jnp.dot(a, b, preferred_element_type=f32)


def dot3(x, w):
    return mm(
        jnp.concatenate([x[0], x[0], x[1]], axis=1), jnp.concatenate([w[0], w[1], w[0]], axis=0)
    )


def layer_norm(values):
    center = values - jnp.mean(values, axis=-1, keepdims=True)
    spread = jnp.mean(center * center, axis=-1, keepdims=True)
    return center * lax.rsqrt(spread + epsilon)


def pick(links, table, base):
    rows, count = links.shape[0], table[0].shape[0]
    lanes = lax.broadcasted_iota(jnp.int32, (rows, count), 1)
    hot = jnp.concatenate(
        [
            jnp.where(lanes == links[:, k : k + 1] - base, 1.0, 0.0).astype(bf16)
            for k in range(links.shape[1])
        ],
        axis=0,
    )
    return mm(jnp.concatenate([hot, hot], axis=1), jnp.concatenate(table, axis=0))


def hidden_sum(picked, receiver):
    rows = receiver.shape[0]
    total = None
    for k in range(picked.shape[0] // rows):
        h = picked[k * rows : (k + 1) * rows] + receiver
        term = h + h * jnp.tanh(h)
        total = term if total is None else total + term
    return total


def kernel(
    n_parts,
    n_patch,
    n_sub,
    n_lvl,
    rim,
    tile,
    nodes_hbm,
    coarse_hbm,
    us_hbm, ur_hbm, uo_hbm,
    cs_hbm, cr_hbm, co_hbm,
    ds_hbm, dr_hbm, do_hbm,
    bs_hbm, br_hbm, bo_hbm,
    children, down_sources, bottom_links, coarse_links,
    ub, ug, cb, cg, db, dg, bb, bg,
    out_nodes,
    out_coarse,
    ns, cs, w_in, w_mid, full_in, full_out, pair_in, pair_out, bias,
    ns_pair, rd, rb, nd, ext, near, hidden, links_out, links_in, coarse_ext,
    table, parts,
    load_sem, x_send, x_recv, y_send, y_recv, c_send, c_recv, bias_send, bias_recv,
    part_send, part_recv, tab_send, tab_recv, rel_send, rel_recv,
    node_send, node_recv, link_send, link_recv, halo_send, halo_recv,
):
    part = lax.axis_index("parts")
    patch = lax.axis_index("patch")
    sub = lax.axis_index("sub")
    lvl = lax.axis_index("lvl")
    rows = nd.shape[0] - 2 * rim
    inner = slice(rim, rim + rows)
    width = table.shape[2]
    tiles = rows // tile
    block = patch * n_lvl + lvl
    blocks = n_patch * n_lvl

    def at_part(o):
        return {"parts": lax.rem(part + o, n_parts)}

    def at_sub(o):
        return {"sub": lax.rem(sub + o, n_sub)}

    def at_lvl(o):
        return {"lvl": lax.rem(lvl + o, n_lvl)}

    def at_patch(o):
        return {"patch": lax.rem(patch + o, n_patch)}

    def at_block(o):
        other = lax.rem(block + o + blocks, blocks)
        return {"patch": other // n_lvl, "lvl": lax.rem(other, n_lvl)}

    pairing = 2 if n_patch % 2 == 0 else 1
    in_pair = lax.rem(patch, pairing)
    group = [(p, z) for z in range(pairing) for p in range(n_parts) if p or z]

    def at_group(d):
        other = patch + 1 - 2 * in_pair if d[1] else patch
        return {"parts": lax.rem(part + d[0], n_parts), "patch": other}

    def from_group(d):
        other = 1 - in_pair if d[1] else in_pair
        return lax.rem(part - d[0] + n_parts, n_parts), other

    def from_sub(o):
        return lax.rem(sub - o + n_sub, n_sub)

    def from_patch(o):
        return lax.rem(patch - o + n_patch, n_patch)

    def from_lvl(o):
        return lax.rem(lvl - o + n_lvl, n_lvl)

    def remote(src, dst, send, recv, device):
        return pltpu.make_async_remote_copy(
            src_ref=src, dst_ref=dst, send_sem=send, recv_sem=recv,
            device_id=device, device_id_type=MESH,
        )

    shared = (dr_hbm, ds_hbm, do_hbm, bs_hbm, br_hbm, bo_hbm)
    place = (
        full_in.at[0], full_in.at[1], full_out.at[0], full_in.at[2], full_in.at[3], full_out.at[1],
    )
    pairs = (
        pair_in.at[0], pair_in.at[1], pair_out.at[0], pair_in.at[2], pair_in.at[3], pair_out.at[1],
    )
    DR, DS, DO, BS, BR, BO = range(6)
    paired = (BS, BR, BO)

    plan = [
        (us_hbm, w_in.at[0]), (nodes_hbm, ns.at[inner]), (ur_hbm, w_in.at[1]), (coarse_hbm, cs),
        (uo_hbm, w_mid.at[0]), (cs_hbm, w_in.at[2]), (cr_hbm, w_in.at[3]), (co_hbm, w_mid.at[1]),
    ]
    plan += [(shared[w], place[w].at[sub]) for w in range(6)]
    loads = [
        pltpu.make_async_copy(src, dst, load_sem.at[i]) for i, (src, dst) in enumerate(plan)
    ]
    for load in loads:
        load.start()
    l_us, l_ns, l_ur, l_cst, l_uo, l_cs, l_cr, l_co = loads[:8]
    l_own = loads[8:]

    barrier = pltpu.get_barrier_semaphore()
    peers = [at_sub(o) for o in range(1, n_sub)]
    peers += [at_part(o) for o in range(1, n_parts)]
    peers += [at_lvl(o) for o in range(1, n_lvl)]
    peers += [at_patch(o) for o in range(1, n_patch)]
    peers += [at_block(-1), at_block(1)]
    peers += [at_group(d) for d in group[n_parts - 1 :] if d[0]]
    for peer in peers:
        pl.semaphore_signal(barrier, inc=1, device_id=peer, device_id_type=MESH)

    def piece_of(w, core, holder):
        side, pair = holder
        count = n_parts * pairing if w in paired else n_parts
        index = core * count + (side * pairing + pair if w in paired else side)
        size = shared[w].shape[0] // (n_lvl * count)
        return pl.ds(pl.multiple_of(index * size, size), size)

    def x_copy(w, o, owner):
        mine = piece_of(w, lvl, (part, in_pair))
        return remote(
            place[w].at[sub, mine], place[w].at[owner, mine],
            x_send.at[w, o - 1], x_recv.at[w, o - 1], at_sub(o),
        )

    def y_copy(w, o, q, holder):
        ref = place[w].at[from_sub(o), piece_of(w, lvl, holder)]
        return remote(
            ref, ref, y_send.at[w, o - 1, q], y_recv.at[w, o - 1, q], at_group(group[q])
        )

    def ways(w):
        return range(len(group) if w in paired else n_parts - 1)

    def c_copy(w, o, q, holder):
        size = shared[w].shape[0] // n_lvl
        piece = pl.ds(pl.multiple_of(holder * size, size), size)
        ref = place[w].at[from_sub(o), piece]
        return remote(ref, ref, c_send.at[w, o - 1, q - 1], c_recv.at[w, o - 1, q - 1], at_lvl(q))

    def start_x(w):
        for o in range(1, n_sub):
            x_copy(w, o, sub).start()

    def forward_y(w):
        for o in range(1, n_sub):
            x_copy(w, o, from_sub(o)).wait_recv()
            for q in ways(w):
                y_copy(w, o, q, (part, in_pair)).start()

    def forward_c(w):
        for o in range(1, n_sub):
            for q in ways(w):
                y_copy(w, o, q, from_group(group[q])).wait_recv()
            for q in range(1, n_lvl):
                c_copy(w, o, q, lvl).start()

    def store_pair(w, s):
        high, low = split(place[w][s])
        pairs[w][s, 0] = high
        pairs[w][s, 1] = low

    def own(w):
        store_pair(w, sub)

    def take(w):
        for o in range(1, n_sub):
            for q in range(1, n_lvl):
                c_copy(w, o, q, from_lvl(q)).wait_recv()
        for o in range(1, n_sub):
            store_pair(w, from_sub(o))

    def bias_copy(o, owner):
        return remote(
            bias.at[owner], bias.at[owner], bias_send.at[o - 1], bias_recv.at[o - 1], at_sub(o)
        )

    def part_copy(j, o, index):
        return remote(
            parts.at[j, index], parts.at[j, index],
            part_send.at[j, o - 1], part_recv.at[j, o - 1], at_sub(o),
        )

    def send_part(j):
        for o in range(1, n_sub):
            part_copy(j, o, sub).start()

    def total_part(j):
        for o in range(1, n_sub):
            part_copy(j, o, from_sub(o)).wait_recv()
        total = parts[j, 0]
        for s in range(1, n_sub):
            total = total + parts[j, s]
        return total

    l_us.wait()
    l_ns.wait()
    high, low = split(ns[inner])
    ns_pair[0, inner] = high
    ns_pair[1, inner] = low
    sender = split(0.5 * dot3((high, low), split(w_in[0])))
    l_ur.wait()
    l_cst.wait()
    receiver = 0.5 * (dot3(split(cs[...]), split(w_in[1])) + ub[...])
    hid = hidden_sum(pick(jnp.transpose(children[...]), sender, 0), receiver)
    l_uo.wait()
    parts[0, sub] = dot3(split(hid), split(w_mid[0]))
    bias[sub, 0:1] = db[...]
    bias[sub, 1:2] = bb[...]

    links_out[...] = jnp.zeros_like(links_out)
    links_out[: down_sources.shape[0]] = down_sources[...]

    def node_copy(side):
        origin = slice(rim, 2 * rim) if side == 0 else slice(rows, rows + rim)
        target = slice(rim + rows, rows + 2 * rim) if side == 0 else slice(0, rim)
        return remote(
            ns.at[origin], ns.at[target], node_send.at[side], node_recv.at[side],
            at_block(2 * side - 1),
        )

    def link_copy(side):
        source = slice(0, rim) if side == 0 else slice(rows - rim, rows)
        return remote(
            links_out.at[:, source], links_in.at[1 - side], link_send.at[side],
            link_recv.at[side], at_block(2 * side - 1),
        )

    def halo_copy(side):
        return remote(
            coarse_ext.at[1], coarse_ext.at[2 - 2 * side], halo_send.at[side], halo_recv.at[side],
            at_block(2 * side - 1),
        )

    for load in l_own:
        load.wait()
    pl.semaphore_wait(barrier, len(peers))
    send_part(0)
    for o in range(1, n_sub):
        bias_copy(o, sub).start()
    for side in range(2):
        link_copy(side).start()
    node_copy(0).start()
    start_x(DR)
    start_x(DS)

    def receive_down(s, piece):
        value = dot3(
            (ns_pair[0, piece], ns_pair[1, piece]), (pair_in[0, s, 0], pair_in[0, s, 1])
        )
        rd[s, piece] = 0.5 * (value + bias[s, 0:1])

    own(DR)
    receive_down(sub, inner)
    near[:, : bottom_links.shape[0]] = jnp.transpose(bottom_links[...])
    l_cs.wait()
    l_cr.wait()
    w_send = split(w_in[2])
    coarse_up = cs[...] + ug[...] * layer_norm(total_part(0))

    up_pair = split(coarse_up)
    table[block] = 0.5 * dot3(up_pair, w_send)

    def tab_copy(o, index):
        return remote(
            table.at[index], table.at[index], tab_send.at[o - 1], tab_recv.at[o - 1], at_patch(o)
        )

    def rel_copy(o, q, index):
        return remote(
            table.at[index], table.at[index],
            rel_send.at[o, q - 1], rel_recv.at[o, q - 1], at_lvl(q),
        )

    order = sorted(range(1, n_patch), key=lambda o: min(o, n_patch - o))
    for o in order:
        tab_copy(o, block).start()
    for q in range(1, n_lvl):
        rel_copy(0, q, block).start()
    receiver = 0.5 * (dot3(up_pair, split(w_in[3])) + cb[...])
    for w in (DS, DO, BS, BR, BO):
        own(w)
    forward_y(DR)
    start_x(DO)
    outer = (slice(0, rim), slice(rim + rows, rows + 2 * rim))

    def take_nodes(side):
        node_copy(1 - side).wait_recv()
        link_copy(1 - side).wait_recv()
        high, low = split(ns[outer[side]])
        ns_pair[0, outer[side]] = high
        ns_pair[1, outer[side]] = low
        receive_down(sub, outer[side])

    take_nodes(1)
    for o in range(1, n_sub):
        bias_copy(o, from_sub(o)).wait_recv()
    forward_y(DS)
    start_x(BS)
    for o in order:
        tab_copy(o, from_patch(o) * n_lvl + lvl).wait_recv()
        for q in range(1, n_lvl):
            rel_copy(o, q, from_patch(o) * n_lvl + lvl).start()
    for q in range(1, n_lvl):
        rel_copy(0, q, patch * n_lvl + from_lvl(q)).wait_recv()
    for o in order:
        for q in range(1, n_lvl):
            rel_copy(o, q, from_patch(o) * n_lvl + from_lvl(q)).wait_recv()

    node_copy(1).start()
    start_x(BR)
    cells = table.shape[1]
    chunk = max(d for d in range(1, blocks + 1) if blocks % d == 0 and d * cells <= 512)
    coarse_columns = jnp.transpose(coarse_links[...])
    picked = None
    for c in range(0, blocks, chunk):
        rows_pair = split(table[c : c + chunk].reshape(chunk * cells, width))
        got = pick(coarse_columns, rows_pair, c * cells)
        picked = got if picked is None else picked + got
    hid = hidden_sum(picked, receiver)
    l_co.wait()
    parts[1, sub] = dot3(split(hid), split(w_mid[1]))
    send_part(1)
    forward_c(DR)
    forward_y(DO)
    forward_y(BS)
    start_x(BO)
    forward_c(DS)
    take(DR)
    for o in range(1, n_sub):
        receive_down(from_sub(o), inner)
        receive_down(from_sub(o), outer[1])
    take(DS)
    forward_y(BR)
    new_coarse = coarse_up + cg[...] * layer_norm(total_part(1))
    coarse_ext[1] = new_coarse
    for side in range(2):
        halo_copy(side).start()
    out_coarse[...] = new_coarse
    forward_c(DO)
    forward_c(BS)
    take(DO)

    def whole(ref, k, axis):
        return jnp.concatenate([ref[s, k] for s in range(n_sub)], axis=axis)

    down_columns = jnp.transpose(links_out[...])

    def down_table(i):
        w_send = (whole(pair_in.at[1], 0, 1), whole(pair_in.at[1], 1, 1))
        return jnp.concatenate(split(0.5 * dot3(split(coarse_ext[i]), w_send)), axis=0)

    def descend(t, count, columns, rows_pair):
        piece = slice(t * tile, (t + count) * tile)
        lanes = lax.rem(
            lax.broadcasted_iota(jnp.int32, (count * tile, 2 * cells), 1), cells
        )
        hot = jnp.concatenate(
            [
                jnp.where(lanes == columns[:, k : k + 1], 1.0, 0.0).astype(bf16)
                for k in range(down_sources.shape[0])
            ],
            axis=0,
        )
        receiver = jnp.concatenate([rd[s, piece] for s in range(n_sub)], axis=1)
        hid = hidden_sum(mm(hot, rows_pair), receiver)
        w_out = (whole(pair_out.at[0], 0, 0), whole(pair_out.at[0], 1, 0))
        nd[piece] = ns[piece] + dg[...] * layer_norm(dot3(split(hid), w_out))

    def project(t, count):
        piece = slice(t * tile, (t + count) * tile)
        w_send = (whole(pair_in.at[2], 0, 1), whole(pair_in.at[2], 1, 1))
        high, low = split(0.5 * dot3(split(nd[piece]), w_send))
        ext[0, piece] = high
        ext[1, piece] = low

    def receive_bottom():
        w_receive = (whole(pair_in.at[3], 0, 1), whole(pair_in.at[3], 1, 1))
        both = jnp.concatenate([bias[s, 1:2] for s in range(n_sub)], axis=1)
        rb[...] = 0.5 * (dot3(split(nd[inner]), w_receive) + both)

    def bottom(t):
        piece = slice(t * tile, (t + 1) * tile)
        window = slice(t * tile, (t + 1) * tile + 2 * rim)
        picked = pick(
            near[piece, : bottom_links.shape[0]], (ext[0, window], ext[1, window]), t * tile
        )
        hidden[piece] = hidden_sum(picked, rb[piece])

    def finish():
        w_out = (whole(pair_out.at[1], 0, 0), whole(pair_out.at[1], 1, 0))
        update = layer_norm(dot3(split(hidden[...]), w_out))
        out_nodes[...] = nd[inner] + bg[...] * update

    rows_pair = down_table(1)
    descend(1, tiles, down_columns, rows_pair)
    take_nodes(0)
    for o in range(1, n_sub):
        receive_down(from_sub(o), outer[0])
    forward_y(BO)
    take(BS)
    project(1, tiles)
    for side in range(2):
        halo_copy(1 - side).wait_recv()
        end = side * (tiles + 1)
        descend(end, 1, jnp.transpose(links_in[side]), down_table(2 * side))
        project(end, 1)
    forward_c(BR)
    take(BR)
    receive_bottom()
    for i, t in enumerate(list(range(1, tiles - 1)) + [0, tiles - 1]):
        bottom(t)
        if i == 0:
            forward_c(BO)
    take(BO)
    finish()

    for o in range(1, n_sub):
        for w in range(6):
            x_copy(w, o, sub).wait_send()
            for q in ways(w):
                y_copy(w, o, q, (part, in_pair)).wait_send()
            for q in range(1, n_lvl):
                c_copy(w, o, q, lvl).wait_send()
        bias_copy(o, sub).wait_send()
        for j in range(2):
            part_copy(j, o, sub).wait_send()
    for o in order:
        tab_copy(o, block).wait_send()
        for q in range(1, n_lvl):
            rel_copy(o, q, from_patch(o) * n_lvl + lvl).wait_send()
    for q in range(1, n_lvl):
        rel_copy(0, q, block).wait_send()
    for side in range(2):
        node_copy(side).wait_send()
        link_copy(side).wait_send()
        halo_copy(side).wait_send()


def hand_over(nodes, coarse, out_nodes, out_coarse):
    out_nodes[...] = nodes[...]
    out_coarse[...] = coarse[...]


def body(
    node_states, coarse_states, children, down_sources, bottom_links, coarse_links,
    upward_sender, upward_receiver, upward_bias, upward_output, upward_gain,
    coarse_sender, coarse_receiver, coarse_bias, coarse_output, coarse_gain,
    downward_sender, downward_receiver, downward_bias, downward_output, downward_gain,
    bottom_sender, bottom_receiver, bottom_bias, bottom_output, bottom_gain,
):
    n_parts, n_patch, n_sub, n_lvl = (
        lax.axis_size(a) for a in ("parts", "patch", "sub", "lvl")
    )
    rows, lat = node_states.shape
    cells = coarse_states.shape[0]
    width = upward_sender.shape[1]
    hid = width * n_sub
    rim = rows // 4
    tile = rim
    blocks = n_patch * n_lvl
    subs, others, cores = max(n_sub - 1, 1), max(2 * n_parts - 1, 1), max(n_lvl - 1, 1)
    row = lambda v: v.reshape(1, -1)
    dma = pltpu.SemaphoreType.DMA
    vmem = pl.BlockSpec(memory_space=pltpu.VMEM)
    anywhere = pl.BlockSpec(memory_space=pl.ANY)
    swept = pl.pallas_call(
        functools.partial(kernel, n_parts, n_patch, n_sub, n_lvl, rim, tile),
        out_shape=(
            jax.ShapeDtypeStruct((rows, lat), f32),
            jax.ShapeDtypeStruct((cells, lat), f32),
        ),
        in_specs=[anywhere] * 14 + [vmem] * 12,
        out_specs=(vmem, vmem),
        scratch_shapes=[
            pltpu.VMEM((rows + 2 * rim, lat), f32),
            pltpu.VMEM((cells, lat), f32),
            pltpu.VMEM((4, lat, width), f32),
            pltpu.VMEM((2, width, lat), f32),
            pltpu.VMEM((4, n_sub, lat, width), f32),
            pltpu.VMEM((2, n_sub, width, lat), f32),
            pltpu.VMEM((4, n_sub, 2, lat, width), bf16),
            pltpu.VMEM((2, n_sub, 2, width, lat), bf16),
            pltpu.VMEM((n_sub, 8, width), f32),
            pltpu.VMEM((2, rows + 2 * rim, lat), bf16),
            pltpu.VMEM((n_sub, rows + 2 * rim, width), f32),
            pltpu.VMEM((rows, hid), f32),
            pltpu.VMEM((rows + 2 * rim, lat), f32),
            pltpu.VMEM((2, rows + 2 * rim, hid), bf16),
            pltpu.VMEM((rows, 128), jnp.int32),
            pltpu.VMEM((rows, hid), f32),
            pltpu.VMEM((8, rows), jnp.int32),
            pltpu.VMEM((2, 8, rim), jnp.int32),
            pltpu.VMEM((3, cells, lat), f32),
            pltpu.VMEM((blocks, cells, width), f32),
            pltpu.VMEM((2, n_sub, cells, lat), f32),
            dma((14,)),
            dma((6, subs)),
            dma((6, subs)),
            dma((6, subs, others)),
            dma((6, subs, others)),
            dma((6, subs, cores)),
            dma((6, subs, cores)),
            dma((subs,)),
            dma((subs,)),
            dma((2, subs)),
            dma((2, subs)),
            dma((n_patch,)),
            dma((n_patch,)),
            dma((n_patch, cores)),
            dma((n_patch, cores)),
            dma((2,)),
            dma((2,)),
            dma((2,)),
            dma((2,)),
            dma((2,)),
            dma((2,)),
        ],
        compiler_params=pltpu.CompilerParams(
            collective_id=0, has_side_effects=True, vmem_limit_bytes=60 * 1024 * 1024
        ),
        name="sweep",
    )(
        node_states, coarse_states,
        upward_sender, upward_receiver, upward_output,
        coarse_sender, coarse_receiver, coarse_output,
        downward_sender, downward_receiver, downward_output,
        bottom_sender, bottom_receiver, bottom_output,
        children.T, down_sources.T, bottom_links.T, coarse_links.T,
        row(upward_bias), row(upward_gain), row(coarse_bias), row(coarse_gain),
        row(downward_bias), row(downward_gain), row(bottom_bias), row(bottom_gain),
    )
    steps = 2
    specs = [pl.BlockSpec((n // steps, lat), lambda i: (i, 0)) for n in (rows, cells)]
    return pl.pallas_call(
        hand_over,
        grid=(steps,),
        out_shape=tuple(jax.ShapeDtypeStruct(v.shape, v.dtype) for v in swept),
        in_specs=specs,
        out_specs=tuple(specs),
        name="hand_over",
    )(*swept)


def solution(mesh):
    rows = P(("parts", "patch", "lvl"), None)
    links = P(("patch", "lvl"), None)
    weights = (P(None, "sub"), P(None, "sub"), P("sub"), P("sub", None), P())
    in_specs = (rows, rows, links, links, links, links) + weights * 4
    return jax.shard_map(
        body, mesh=mesh, in_specs=in_specs, out_specs=(rows, rows), check_vma=False
    )
```

```python
import functools

import jax
import jax.numpy as jnp
from jax import lax
from jax.experimental import pallas as pl
from jax.experimental.pallas import tpu as pltpu
from jax.sharding import PartitionSpec as P

epsilon = 1e-05
f32 = jnp.float32
bf16 = jnp.bfloat16
MESH = pl.DeviceIdType.MESH


def split(x):
    high = x.astype(bf16)
    return high, (x - high.astype(f32)).astype(bf16)


def mm(a, b):
    return jnp.dot(a, b, preferred_element_type=f32)


def dot3(x, w):
    return mm(
        jnp.concatenate([x[0], x[0], x[1]], axis=1), jnp.concatenate([w[0], w[1], w[0]], axis=0)
    )


def layer_norm(values):
    center = values - jnp.mean(values, axis=-1, keepdims=True)
    spread = jnp.mean(center * center, axis=-1, keepdims=True)
    return center * lax.rsqrt(spread + epsilon)


def pick(links, table, base):
    rows, count = links.shape[0], table[0].shape[0]
    lanes = lax.broadcasted_iota(jnp.int32, (rows, count), 1)
    hot = jnp.concatenate(
        [
            jnp.where(lanes == links[:, k : k + 1] - base, 1.0, 0.0).astype(bf16)
            for k in range(links.shape[1])
        ],
        axis=0,
    )
    return mm(jnp.concatenate([hot, hot], axis=1), jnp.concatenate(table, axis=0))


def hidden_sum(picked, receiver):
    rows = receiver.shape[0]
    total = None
    for k in range(picked.shape[0] // rows):
        h = picked[k * rows : (k + 1) * rows] + receiver
        term = h + h * jnp.tanh(h)
        total = term if total is None else total + term
    return total


def kernel(
    n_parts,
    n_patch,
    n_sub,
    n_lvl,
    rim,
    tile,
    nodes_hbm,
    coarse_hbm,
    us_hbm, ur_hbm, uo_hbm,
    cs_hbm, cr_hbm, co_hbm,
    ds_hbm, dr_hbm, do_hbm,
    bs_hbm, br_hbm, bo_hbm,
    children, down_sources, bottom_links, coarse_links,
    ub, ug, cb, cg, db, dg, bb, bg,
    out_nodes,
    out_coarse,
    ns, cs, w_in, w_mid, full_in, full_out, pair_in, pair_out, bias,
    ns_pair, rd, rb, nd, ext, near, hidden, links_out, links_in, coarse_ext,
    table, parts,
    load_sem, x_send, x_recv, y_send, y_recv, c_send, c_recv, bias_send, bias_recv,
    part_send, part_recv, tab_send, tab_recv, rel_send, rel_recv,
    node_send, node_recv, link_send, link_recv, halo_send, halo_recv,
):
    part = lax.axis_index("parts")
    patch = lax.axis_index("patch")
    sub = lax.axis_index("sub")
    lvl = lax.axis_index("lvl")
    rows = nd.shape[0] - 2 * rim
    inner = slice(rim, rim + rows)
    width = table.shape[2]
    tiles = rows // tile
    block = patch * n_lvl + lvl
    blocks = n_patch * n_lvl

    def at_part(o):
        return {"parts": lax.rem(part + o, n_parts)}

    def at_sub(o):
        return {"sub": lax.rem(sub + o, n_sub)}

    def at_lvl(o):
        return {"lvl": lax.rem(lvl + o, n_lvl)}

    def at_patch(o):
        return {"patch": lax.rem(patch + o, n_patch)}

    def at_block(o):
        other = lax.rem(block + o + blocks, blocks)
        return {"patch": other // n_lvl, "lvl": lax.rem(other, n_lvl)}

    pairing = 2 if n_patch % 2 == 0 else 1
    in_pair = lax.rem(patch, pairing)
    group = [(p, z) for z in range(pairing) for p in range(n_parts) if p or z]

    def at_group(d):
        other = patch + 1 - 2 * in_pair if d[1] else patch
        return {"parts": lax.rem(part + d[0], n_parts), "patch": other}

    def from_group(d):
        other = 1 - in_pair if d[1] else in_pair
        return lax.rem(part - d[0] + n_parts, n_parts), other

    def from_sub(o):
        return lax.rem(sub - o + n_sub, n_sub)

    def from_patch(o):
        return lax.rem(patch - o + n_patch, n_patch)

    def from_lvl(o):
        return lax.rem(lvl - o + n_lvl, n_lvl)

    def remote(src, dst, send, recv, device):
        return pltpu.make_async_remote_copy(
            src_ref=src, dst_ref=dst, send_sem=send, recv_sem=recv,
            device_id=device, device_id_type=MESH,
        )

    shared = (dr_hbm, ds_hbm, do_hbm, bs_hbm, br_hbm, bo_hbm)
    place = (
        full_in.at[0], full_in.at[1], full_out.at[0], full_in.at[2], full_in.at[3], full_out.at[1],
    )
    pairs = (
        pair_in.at[0], pair_in.at[1], pair_out.at[0], pair_in.at[2], pair_in.at[3], pair_out.at[1],
    )
    DR, DS, DO, BS, BR, BO = range(6)
    paired = (BS, BR, BO)

    plan = [
        (us_hbm, w_in.at[0]), (nodes_hbm, ns.at[inner]), (ur_hbm, w_in.at[1]), (coarse_hbm, cs),
        (uo_hbm, w_mid.at[0]), (cs_hbm, w_in.at[2]), (cr_hbm, w_in.at[3]), (co_hbm, w_mid.at[1]),
    ]
    plan += [(shared[w], place[w].at[sub]) for w in range(6)]
    loads = [
        pltpu.make_async_copy(src, dst, load_sem.at[i]) for i, (src, dst) in enumerate(plan)
    ]
    for load in loads:
        load.start()
    l_us, l_ns, l_ur, l_cst, l_uo, l_cs, l_cr, l_co = loads[:8]
    l_own = loads[8:]

    barrier = pltpu.get_barrier_semaphore()
    peers = [at_sub(o) for o in range(1, n_sub)]
    peers += [at_part(o) for o in range(1, n_parts)]
    peers += [at_lvl(o) for o in range(1, n_lvl)]
    peers += [at_patch(o) for o in range(1, n_patch)]
    peers += [at_block(-1), at_block(1)]
    peers += [at_group(d) for d in group[n_parts - 1 :] if d[0]]
    for peer in peers:
        pl.semaphore_signal(barrier, inc=1, device_id=peer, device_id_type=MESH)

    def piece_of(w, core, holder):
        side, pair = holder
        count = n_parts * pairing if w in paired else n_parts
        index = core * count + (side * pairing + pair if w in paired else side)
        size = shared[w].shape[0] // (n_lvl * count)
        return pl.ds(pl.multiple_of(index * size, size), size)

    def x_copy(w, o, owner):
        mine = piece_of(w, lvl, (part, in_pair))
        return remote(
            place[w].at[sub, mine], place[w].at[owner, mine],
            x_send.at[w, o - 1], x_recv.at[w, o - 1], at_sub(o),
        )

    def y_copy(w, o, q, holder):
        ref = place[w].at[from_sub(o), piece_of(w, lvl, holder)]
        return remote(
            ref, ref, y_send.at[w, o - 1, q], y_recv.at[w, o - 1, q], at_group(group[q])
        )

    def ways(w):
        return range(len(group) if w in paired else n_parts - 1)

    def c_copy(w, o, q, holder):
        size = shared[w].shape[0] // n_lvl
        piece = pl.ds(pl.multiple_of(holder * size, size), size)
        ref = place[w].at[from_sub(o), piece]
        return remote(ref, ref, c_send.at[w, o - 1, q - 1], c_recv.at[w, o - 1, q - 1], at_lvl(q))

    def start_x(w):
        for o in range(1, n_sub):
            x_copy(w, o, sub).start()

    def forward_y(w):
        for o in range(1, n_sub):
            x_copy(w, o, from_sub(o)).wait_recv()
            for q in ways(w):
                y_copy(w, o, q, (part, in_pair)).start()

    def forward_c(w):
        for o in range(1, n_sub):
            for q in ways(w):
                y_copy(w, o, q, from_group(group[q])).wait_recv()
            for q in range(1, n_lvl):
                c_copy(w, o, q, lvl).start()

    def store_pair(w, s):
        high, low = split(place[w][s])
        pairs[w][s, 0] = high
        pairs[w][s, 1] = low

    def own(w):
        store_pair(w, sub)

    def take(w):
        for o in range(1, n_sub):
            for q in range(1, n_lvl):
                c_copy(w, o, q, from_lvl(q)).wait_recv()
        for o in range(1, n_sub):
            store_pair(w, from_sub(o))

    def bias_copy(o, owner):
        return remote(
            bias.at[owner], bias.at[owner], bias_send.at[o - 1], bias_recv.at[o - 1], at_sub(o)
        )

    def part_copy(j, o, index):
        return remote(
            parts.at[j, index], parts.at[j, index],
            part_send.at[j, o - 1], part_recv.at[j, o - 1], at_sub(o),
        )

    def send_part(j):
        for o in range(1, n_sub):
            part_copy(j, o, sub).start()

    def total_part(j):
        for o in range(1, n_sub):
            part_copy(j, o, from_sub(o)).wait_recv()
        total = parts[j, 0]
        for s in range(1, n_sub):
            total = total + parts[j, s]
        return total

    l_us.wait()
    l_ns.wait()
    high, low = split(ns[inner])
    ns_pair[0, inner] = high
    ns_pair[1, inner] = low
    sender = split(0.5 * dot3((high, low), split(w_in[0])))
    l_ur.wait()
    l_cst.wait()
    receiver = 0.5 * (dot3(split(cs[...]), split(w_in[1])) + ub[...])
    hid = hidden_sum(pick(jnp.transpose(children[...]), sender, 0), receiver)
    l_uo.wait()
    parts[0, sub] = dot3(split(hid), split(w_mid[0]))
    bias[sub, 0:1] = db[...]
    bias[sub, 1:2] = bb[...]

    links_out[...] = jnp.zeros_like(links_out)
    links_out[: down_sources.shape[0]] = down_sources[...]

    def node_copy(side):
        origin = slice(rim, 2 * rim) if side == 0 else slice(rows, rows + rim)
        target = slice(rim + rows, rows + 2 * rim) if side == 0 else slice(0, rim)
        return remote(
            ns.at[origin], ns.at[target], node_send.at[side], node_recv.at[side],
            at_block(2 * side - 1),
        )

    def link_copy(side):
        source = slice(0, rim) if side == 0 else slice(rows - rim, rows)
        return remote(
            links_out.at[:, source], links_in.at[1 - side], link_send.at[side],
            link_recv.at[side], at_block(2 * side - 1),
        )

    def halo_copy(side):
        return remote(
            coarse_ext.at[1], coarse_ext.at[2 - 2 * side], halo_send.at[side], halo_recv.at[side],
            at_block(2 * side - 1),
        )

    for load in l_own:
        load.wait()
    pl.semaphore_wait(barrier, len(peers))
    send_part(0)
    for o in range(1, n_sub):
        bias_copy(o, sub).start()
    for side in range(2):
        link_copy(side).start()
    node_copy(0).start()
    start_x(DR)
    start_x(DS)

    def receive_down(s, piece):
        value = dot3(
            (ns_pair[0, piece], ns_pair[1, piece]), (pair_in[0, s, 0], pair_in[0, s, 1])
        )
        rd[s, piece] = 0.5 * (value + bias[s, 0:1])

    own(DR)
    receive_down(sub, inner)
    near[:, : bottom_links.shape[0]] = jnp.transpose(bottom_links[...])
    l_cs.wait()
    l_cr.wait()
    w_send = split(w_in[2])
    coarse_up = cs[...] + ug[...] * layer_norm(total_part(0))

    up_pair = split(coarse_up)
    table[block] = 0.5 * dot3(up_pair, w_send)

    def tab_copy(o, index):
        return remote(
            table.at[index], table.at[index], tab_send.at[o - 1], tab_recv.at[o - 1], at_patch(o)
        )

    def rel_copy(o, q, index):
        return remote(
            table.at[index], table.at[index],
            rel_send.at[o, q - 1], rel_recv.at[o, q - 1], at_lvl(q),
        )

    order = sorted(range(1, n_patch), key=lambda o: min(o, n_patch - o))
    for o in reversed(order):
        tab_copy(o, block).start()
    for q in range(1, n_lvl):
        rel_copy(0, q, block).start()
    receiver = 0.5 * (dot3(up_pair, split(w_in[3])) + cb[...])
    for w in (DS, DO, BS, BR, BO):
        own(w)
    forward_y(DR)
    start_x(DO)
    outer = (slice(0, rim), slice(rim + rows, rows + 2 * rim))

    def take_nodes(side):
        node_copy(1 - side).wait_recv()
        link_copy(1 - side).wait_recv()
        high, low = split(ns[outer[side]])
        ns_pair[0, outer[side]] = high
        ns_pair[1, outer[side]] = low
        receive_down(sub, outer[side])

    take_nodes(1)
    for o in range(1, n_sub):
        bias_copy(o, from_sub(o)).wait_recv()
    forward_y(DS)
    start_x(BS)
    for o in order:
        tab_copy(o, from_patch(o) * n_lvl + lvl).wait_recv()
        for q in range(1, n_lvl):
            rel_copy(o, q, from_patch(o) * n_lvl + lvl).start()
    for q in range(1, n_lvl):
        rel_copy(0, q, patch * n_lvl + from_lvl(q)).wait_recv()
    for o in order:
        for q in range(1, n_lvl):
            rel_copy(o, q, from_patch(o) * n_lvl + from_lvl(q)).wait_recv()

    node_copy(1).start()
    start_x(BR)
    cells = table.shape[1]
    chunk = max(d for d in range(1, blocks + 1) if blocks % d == 0 and d * cells <= 512)
    coarse_columns = jnp.transpose(coarse_links[...])
    picked = None
    for c in range(0, blocks, chunk):
        rows_pair = split(table[c : c + chunk].reshape(chunk * cells, width))
        got = pick(coarse_columns, rows_pair, c * cells)
        picked = got if picked is None else picked + got
    hid = hidden_sum(picked, receiver)
    l_co.wait()
    parts[1, sub] = dot3(split(hid), split(w_mid[1]))
    send_part(1)
    forward_c(DR)
    forward_y(DO)
    forward_y(BS)
    start_x(BO)
    forward_c(DS)
    take(DR)
    for o in range(1, n_sub):
        receive_down(from_sub(o), inner)
        receive_down(from_sub(o), outer[1])
    take(DS)
    forward_y(BR)
    new_coarse = coarse_up + cg[...] * layer_norm(total_part(1))
    coarse_ext[1] = new_coarse
    for side in range(2):
        halo_copy(side).start()
    out_coarse[...] = new_coarse
    forward_c(DO)
    forward_c(BS)
    take(DO)

    def whole(ref, k, axis):
        return jnp.concatenate([ref[s, k] for s in range(n_sub)], axis=axis)

    down_columns = jnp.transpose(links_out[...])

    def down_table(i):
        w_send = (whole(pair_in.at[1], 0, 1), whole(pair_in.at[1], 1, 1))
        return jnp.concatenate(split(0.5 * dot3(split(coarse_ext[i]), w_send)), axis=0)

    def descend(t, count, columns, rows_pair):
        piece = slice(t * tile, (t + count) * tile)
        lanes = lax.rem(
            lax.broadcasted_iota(jnp.int32, (count * tile, 2 * cells), 1), cells
        )
        hot = jnp.concatenate(
            [
                jnp.where(lanes == columns[:, k : k + 1], 1.0, 0.0).astype(bf16)
                for k in range(down_sources.shape[0])
            ],
            axis=0,
        )
        receiver = jnp.concatenate([rd[s, piece] for s in range(n_sub)], axis=1)
        hid = hidden_sum(mm(hot, rows_pair), receiver)
        w_out = (whole(pair_out.at[0], 0, 0), whole(pair_out.at[0], 1, 0))
        nd[piece] = ns[piece] + dg[...] * layer_norm(dot3(split(hid), w_out))

    def project(t, count):
        piece = slice(t * tile, (t + count) * tile)
        w_send = (whole(pair_in.at[2], 0, 1), whole(pair_in.at[2], 1, 1))
        high, low = split(0.5 * dot3(split(nd[piece]), w_send))
        ext[0, piece] = high
        ext[1, piece] = low

    def receive_bottom():
        w_receive = (whole(pair_in.at[3], 0, 1), whole(pair_in.at[3], 1, 1))
        both = jnp.concatenate([bias[s, 1:2] for s in range(n_sub)], axis=1)
        rb[...] = 0.5 * (dot3(split(nd[inner]), w_receive) + both)

    def bottom(t):
        piece = slice(t * tile, (t + 1) * tile)
        window = slice(t * tile, (t + 1) * tile + 2 * rim)
        picked = pick(
            near[piece, : bottom_links.shape[0]], (ext[0, window], ext[1, window]), t * tile
        )
        hidden[piece] = hidden_sum(picked, rb[piece])

    def finish():
        w_out = (whole(pair_out.at[1], 0, 0), whole(pair_out.at[1], 1, 0))
        update = layer_norm(dot3(split(hidden[...]), w_out))
        out_nodes[...] = nd[inner] + bg[...] * update

    rows_pair = down_table(1)
    descend(1, tiles, down_columns, rows_pair)
    take_nodes(0)
    for o in range(1, n_sub):
        receive_down(from_sub(o), outer[0])
    forward_y(BO)
    take(BS)
    project(1, tiles)
    for side in range(2):
        halo_copy(1 - side).wait_recv()
        end = side * (tiles + 1)
        descend(end, 1, jnp.transpose(links_in[side]), down_table(2 * side))
        project(end, 1)
    forward_c(BR)
    take(BR)
    receive_bottom()
    for i, t in enumerate(list(range(1, tiles - 1)) + [0, tiles - 1]):
        bottom(t)
        if i == 0:
            forward_c(BO)
    take(BO)
    finish()

    for o in range(1, n_sub):
        for w in range(6):
            x_copy(w, o, sub).wait_send()
            for q in ways(w):
                y_copy(w, o, q, (part, in_pair)).wait_send()
            for q in range(1, n_lvl):
                c_copy(w, o, q, lvl).wait_send()
        bias_copy(o, sub).wait_send()
        for j in range(2):
            part_copy(j, o, sub).wait_send()
    for o in order:
        tab_copy(o, block).wait_send()
        for q in range(1, n_lvl):
            rel_copy(o, q, from_patch(o) * n_lvl + lvl).wait_send()
    for q in range(1, n_lvl):
        rel_copy(0, q, block).wait_send()
    for side in range(2):
        node_copy(side).wait_send()
        link_copy(side).wait_send()
        halo_copy(side).wait_send()


def hand_over(nodes, coarse, out_nodes, out_coarse):
    out_nodes[...] = nodes[...]
    out_coarse[...] = coarse[...]


def body(
    node_states, coarse_states, children, down_sources, bottom_links, coarse_links,
    upward_sender, upward_receiver, upward_bias, upward_output, upward_gain,
    coarse_sender, coarse_receiver, coarse_bias, coarse_output, coarse_gain,
    downward_sender, downward_receiver, downward_bias, downward_output, downward_gain,
    bottom_sender, bottom_receiver, bottom_bias, bottom_output, bottom_gain,
):
    n_parts, n_patch, n_sub, n_lvl = (
        lax.axis_size(a) for a in ("parts", "patch", "sub", "lvl")
    )
    rows, lat = node_states.shape
    cells = coarse_states.shape[0]
    width = upward_sender.shape[1]
    hid = width * n_sub
    rim = rows // 4
    tile = rim
    blocks = n_patch * n_lvl
    subs, others, cores = max(n_sub - 1, 1), max(2 * n_parts - 1, 1), max(n_lvl - 1, 1)
    row = lambda v: v.reshape(1, -1)
    dma = pltpu.SemaphoreType.DMA
    vmem = pl.BlockSpec(memory_space=pltpu.VMEM)
    anywhere = pl.BlockSpec(memory_space=pl.ANY)
    swept = pl.pallas_call(
        functools.partial(kernel, n_parts, n_patch, n_sub, n_lvl, rim, tile),
        out_shape=(
            jax.ShapeDtypeStruct((rows, lat), f32),
            jax.ShapeDtypeStruct((cells, lat), f32),
        ),
        in_specs=[anywhere] * 14 + [vmem] * 12,
        out_specs=(vmem, vmem),
        scratch_shapes=[
            pltpu.VMEM((rows + 2 * rim, lat), f32),
            pltpu.VMEM((cells, lat), f32),
            pltpu.VMEM((4, lat, width), f32),
            pltpu.VMEM((2, width, lat), f32),
            pltpu.VMEM((4, n_sub, lat, width), f32),
            pltpu.VMEM((2, n_sub, width, lat), f32),
            pltpu.VMEM((4, n_sub, 2, lat, width), bf16),
            pltpu.VMEM((2, n_sub, 2, width, lat), bf16),
            pltpu.VMEM((n_sub, 8, width), f32),
            pltpu.VMEM((2, rows + 2 * rim, lat), bf16),
            pltpu.VMEM((n_sub, rows + 2 * rim, width), f32),
            pltpu.VMEM((rows, hid), f32),
            pltpu.VMEM((rows + 2 * rim, lat), f32),
            pltpu.VMEM((2, rows + 2 * rim, hid), bf16),
            pltpu.VMEM((rows, 128), jnp.int32),
            pltpu.VMEM((rows, hid), f32),
            pltpu.VMEM((8, rows), jnp.int32),
            pltpu.VMEM((2, 8, rim), jnp.int32),
            pltpu.VMEM((3, cells, lat), f32),
            pltpu.VMEM((blocks, cells, width), f32),
            pltpu.VMEM((2, n_sub, cells, lat), f32),
            dma((14,)),
            dma((6, subs)),
            dma((6, subs)),
            dma((6, subs, others)),
            dma((6, subs, others)),
            dma((6, subs, cores)),
            dma((6, subs, cores)),
            dma((subs,)),
            dma((subs,)),
            dma((2, subs)),
            dma((2, subs)),
            dma((n_patch,)),
            dma((n_patch,)),
            dma((n_patch, cores)),
            dma((n_patch, cores)),
            dma((2,)),
            dma((2,)),
            dma((2,)),
            dma((2,)),
            dma((2,)),
            dma((2,)),
        ],
        compiler_params=pltpu.CompilerParams(
            collective_id=0, has_side_effects=True, vmem_limit_bytes=60 * 1024 * 1024
        ),
        name="sweep",
    )(
        node_states, coarse_states,
        upward_sender, upward_receiver, upward_output,
        coarse_sender, coarse_receiver, coarse_output,
        downward_sender, downward_receiver, downward_output,
        bottom_sender, bottom_receiver, bottom_output,
        children.T, down_sources.T, bottom_links.T, coarse_links.T,
        row(upward_bias), row(upward_gain), row(coarse_bias), row(coarse_gain),
        row(downward_bias), row(downward_gain), row(bottom_bias), row(bottom_gain),
    )
    steps = 2
    specs = [pl.BlockSpec((n // steps, lat), lambda i: (i, 0)) for n in (rows, cells)]
    return pl.pallas_call(
        hand_over,
        grid=(steps,),
        out_shape=tuple(jax.ShapeDtypeStruct(v.shape, v.dtype) for v in swept),
        in_specs=specs,
        out_specs=tuple(specs),
        name="hand_over",
    )(*swept)


def solution(mesh):
    rows = P(("parts", "patch", "lvl"), None)
    links = P(("patch", "lvl"), None)
    weights = (P(None, "sub"), P(None, "sub"), P("sub"), P("sub", None), P())
    in_specs = (rows, rows, links, links, links, links) + weights * 4
    return jax.shard_map(
        body, mesh=mesh, in_specs=in_specs, out_specs=(rows, rows), check_vma=False
    )
```
